256 devices in a mesh: mesh: 64 (over x, z, core), sub: 4 (over y).
Axes of the slice: x: 4, y: 4, z: 8, core: 2. Of those that a mesh axis runs over, the one named last changes fastest.
Arguments:
- coords: float32 [3, 524288], P(None, ('mesh', 'sub')), may hold values from -6 to 6
- veloc: float32 [3, 524288], P(None, ('mesh', 'sub')), may hold values from -6 to 6
- node_mass: float32 [524288], P(('mesh', 'sub')), may hold values from 0.5 to 2
- stress: float32 [3, 1048576], P(None, ('mesh', 'sub')), may hold values from -4 to 4
- connect: int32 [4, 1048576], P(None, ('mesh', 'sub')), may hold values from 0 to 3071
- send_mesh: int32 [131072], P(('mesh', 'sub')), may hold values from 0 to 2047
- send_sub: int32 [131072], P(('mesh', 'sub')), may hold values from 0 to 2047
- send_pick: int32 [4, 32768], P(None, ('mesh', 'sub')), may hold values from 0 to 31
- bucket_list: int32 [4, 4, 4096], P(None, None, ('mesh', 'sub')), may hold values from 0 to 127
- pair_mask: int32 [4, 4, 524288], P(None, None, ('mesh', 'sub')), may hold values 0 or 1
Outputs:
- veloc_out: float32 [3, 524288], P(None, ('mesh', 'sub'))
- stress_out: float32 [3, 1048576], P(None, ('mesh', 'sub'))
The draws below stay inside these ranges and needn't reach their ends.
Inputs may be any that keep to these rules, and one draw needn't show every extreme that they name: `connect`: columns below 2048 are own nodes, then 512 mesh ghosts, then 512 sub ghosts. `send_pick`: a block may be sent to several receivers and several places.
All inputs are finite; a program needn't handle non-finite values. No bound on the sum of `pair_mask` on one device may be relied on, other than what follows from the above.
Results may differ from the reference program's by a relative error of at most 0.0003.
Values sent between devices are 32-bit elements; how exact they have to be, the bound alone decides.
A program may use at most 64 MiB of HBM per device.

```python
import math
import jax
import jax.numpy as jnp
from jax import lax

NODE_DEV = 2048
ELEM_DEV = 4096
GHOST_M = 512
GHOST_S = 512
SEG = 128
CAP = 2
CAND = 4
STEPS = 4
NODES = 524288
ELEMS = 1048576
SLOTS = 128
PICKS = 32768
BUCKETS = 4096
N_MESH = 64
N_SUB = 4


def with_ends(values, key, low, largest):
    index_at = [jax.random.randint(jax.random.fold_in(key, axis), (), 0, length) for axis, length in enumerate(values.shape)]
    main_axis = values.shape.index(max(values.shape))
    beside = index_at[:main_axis] + [(index_at[main_axis] + 1) % values.shape[main_axis]] + index_at[main_axis + 1:]
    return values.at[tuple(index_at)].set(low).at[tuple(beside)].set(largest)


def levels(own_key, extent, shards, least, high):
    factor_of, own = 1.0, jax.random.fold_in(own_key, 6)
    for dim, parts in shards:
        draws = jnp.exp(jax.random.uniform(jax.random.fold_in(own, dim), (parts,), jnp.float32, least / len(shards), high / len(shards)))
        factor_of = factor_of * jnp.repeat(draws, extent[dim] // parts).reshape([-1 if axis == dim else 1 for axis in range(len(extent))])
    return factor_of


def centred(stream_key, dims, width, limit, cuts=(), held_as=jnp.bfloat16):
    drawn = width * jax.random.normal(stream_key, dims, jnp.float32)
    if cuts:
        drawn = drawn * levels(stream_key, dims, cuts, -0.22, 0.18)
    return jnp.clip(drawn, -limit, limit).astype(held_as)


def setup_inputs(seed: int = 0) -> dict:
    keys = jax.random.split(jax.random.key(seed), 11)
    coords = centred(keys[0], (3, NODES), 1.0, 6.0, ((1, 256),), jnp.float32)
    veloc = centred(keys[1], (3, NODES), 1.0, 6.0, ((1, 256),), jnp.float32)
    node_mass = jnp.clip(jnp.exp(math.log(2.0) - 1.3862944 * jax.random.uniform(keys[2], (NODES,), jnp.float32) ** levels(keys[2], (NODES,), ((0, 256),), -0.2, 0.2)), 0.5, 2.0)
    stress = centred(keys[3], (3, ELEMS), 0.5, 4.0, ((1, 256),), jnp.float32)
    connect = with_ends(jax.random.randint(keys[4], (4, ELEMS), 0, NODE_DEV + GHOST_M + GHOST_S), jax.random.fold_in(keys[4], 1), 0, (NODE_DEV + GHOST_M + GHOST_S) - 1).astype(jnp.int32)
    send_mesh = with_ends(jax.random.randint(keys[5], (GHOST_M * N_MESH * N_SUB,), 0, NODE_DEV), jax.random.fold_in(keys[5], 1), 0, NODE_DEV - 1).astype(jnp.int32)
    send_sub = with_ends(jax.random.randint(keys[6], (GHOST_S * N_MESH * N_SUB,), 0, NODE_DEV), jax.random.fold_in(keys[6], 1), 0, NODE_DEV - 1).astype(jnp.int32)
    send_pick = with_ends(jax.random.randint(keys[7], (STEPS, PICKS), 0, ELEM_DEV // SEG), jax.random.fold_in(keys[7], 1), 0, (ELEM_DEV // SEG) - 1).astype(jnp.int32)
    bucket_list = with_ends(jax.random.randint(keys[8], (STEPS, CAND, BUCKETS), 0, SLOTS), jax.random.fold_in(keys[8], 1), 0, SLOTS - 1).astype(jnp.int32)
    pair_mask = with_ends((jax.random.randint(keys[9], (STEPS, CAND, NODES), 0, 2) < 1).astype(jnp.int32), jax.random.fold_in(keys[9], 1), 0, 1)
    return {"coords": coords, "veloc": veloc, "node_mass": node_mass, "stress": stress, "connect": connect, "send_mesh": send_mesh, "send_sub": send_sub, "send_pick": send_pick, "bucket_list": bucket_list, "pair_mask": pair_mask}


TIME_STEP = 0.2
YOUNG = 1.0
POISSON = 0.3
HOURGLASS = 0.01
PENALTY = 0.2
REACH = 4.0
HIGH = lax.Precision.HIGHEST
HOUR_SIGNS = (1.0, -1.0, 1.0, -1.0)

def cross_rows(left_vec, right_vec):
    return jnp.stack([left_vec[1] * right_vec[2] - left_vec[2] * right_vec[1], left_vec[2] * right_vec[0] - left_vec[0] * right_vec[2], left_vec[0] * right_vec[1] - left_vec[1] * right_vec[0]])

def geometry(corner):
    diag_one = corner[:, 2] - corner[:, 0]
    diag_two = corner[:, 3] - corner[:, 1]
    normal_raw = cross_rows(diag_one, diag_two)
    twice_area = jnp.maximum(jnp.sqrt(lax.optimization_barrier(jnp.sum(normal_raw * normal_raw, axis=0))), 1.0)
    normal = normal_raw / twice_area
    centre = 0.25 * (corner[:, 0] + corner[:, 1] + corner[:, 2] + corner[:, 3])
    return (centre, normal, twice_area)

def shell_forces(corner, corner_vel, stress_now):
    centre, normal, twice_area = geometry(corner)
    side_raw = corner[:, 1] - corner[:, 0]
    side_len = jnp.maximum(jnp.sqrt(lax.optimization_barrier(jnp.sum(side_raw * side_raw, axis=0))), 1.0)
    axis_one = side_raw / side_len
    axis_two = cross_rows(normal, axis_one)
    relative = corner - centre[:, None]
    local_x = lax.optimization_barrier(jnp.sum(relative * axis_one[:, None], axis=0))
    local_y = lax.optimization_barrier(jnp.sum(relative * axis_two[:, None], axis=0))
    vel_x = lax.optimization_barrier(jnp.sum(corner_vel * axis_one[:, None], axis=0))
    vel_y = lax.optimization_barrier(jnp.sum(corner_vel * axis_two[:, None], axis=0))
    deriv_x = jnp.stack([local_y[1] - local_y[3], local_y[2] - local_y[0], local_y[3] - local_y[1], local_y[0] - local_y[2]]) / twice_area
    deriv_y = jnp.stack([local_x[3] - local_x[1], local_x[0] - local_x[2], local_x[1] - local_x[3], local_x[2] - local_x[0]]) / twice_area
    rate_xx = lax.optimization_barrier(jnp.sum(deriv_x * vel_x, axis=0))
    rate_yy = lax.optimization_barrier(jnp.sum(deriv_y * vel_y, axis=0))
    rate_xy = lax.optimization_barrier(jnp.sum(deriv_y * vel_x + deriv_x * vel_y, axis=0))
    plane_stiff = YOUNG / (1.0 - POISSON * POISSON)
    stress_new = stress_now + TIME_STEP * jnp.stack([plane_stiff * (rate_xx + POISSON * rate_yy), plane_stiff * (POISSON * rate_xx + rate_yy), YOUNG / (2.0 * (1.0 + POISSON)) * rate_xy])
    half_area = 0.5 * twice_area
    force_x = half_area * (deriv_x * stress_new[0] + deriv_y * stress_new[2])
    force_y = half_area * (deriv_y * stress_new[1] + deriv_x * stress_new[2])
    hour_signs = jnp.array(HOUR_SIGNS, jnp.float32)[:, None]
    hour_x = lax.optimization_barrier(jnp.sum(hour_signs * local_x, axis=0))
    hour_y = lax.optimization_barrier(jnp.sum(hour_signs * local_y, axis=0))
    hour_shape = hour_signs - hour_x * deriv_x - hour_y * deriv_y
    hour_rate = lax.optimization_barrier(jnp.sum(hour_shape[None] * corner_vel, axis=1))
    internal = force_x[None] * axis_one[:, None] + force_y[None] * axis_two[:, None] + HOURGLASS * hour_shape[None] * hour_rate[:, None]
    return (internal, stress_new, centre, normal)

def contact_tiles(slaves, candidates, live_mask):
    centre = candidates[:, :, 0:3]
    normal = candidates[:, :, 3:6]
    offset = slaves[None, :, :, :, None] - centre[:, :, :, None, :]
    gap_depth = lax.optimization_barrier(jnp.sum(offset * normal[:, :, :, None, :], axis=2))
    spread = lax.optimization_barrier(jnp.sum(offset * offset, axis=2)) - gap_depth * gap_depth
    weight = PENALTY * jnp.maximum(-gap_depth, 0.0) * jnp.exp(-spread / REACH) * live_mask[:, :, :, None]
    slave_force = jnp.einsum('kgij,kgcj->gci', weight, normal, precision=HIGH)
    reaction = -normal * lax.optimization_barrier(jnp.sum(weight, axis=2))[:, :, None, :]
    return (slave_force, reaction)

def roll_devices(values_in, amount, axis_pos):
    shaped = values_in.reshape((N_MESH, N_SUB) + values_in.shape[1:])
    return jnp.roll(shaped, amount, axis=axis_pos).reshape(values_in.shape)

def swap_peers(values_in):
    shaped = values_in.reshape((N_MESH, N_SUB, N_MESH, CAP) + values_in.shape[2:])
    order = (2, 1, 0, 3) + tuple(range(4, shaped.ndim))
    return shaped.transpose(order).reshape(values_in.shape)

def reference(coords, veloc, node_mass, stress, connect, send_mesh, send_sub, send_pick, bucket_list, pair_mask):
    devices = N_MESH * N_SUB
    total_nodes = NODE_DEV + GHOST_M + GHOST_S
    bucket_count = NODE_DEV // SEG
    block_count = ELEM_DEV // SEG
    positions = coords.reshape(3, devices, NODE_DEV).transpose(1, 0, 2)
    velocity = veloc.reshape(3, devices, NODE_DEV).transpose(1, 0, 2)
    masses = node_mass.reshape(devices, NODE_DEV)
    stress_now = stress.reshape(3, devices, ELEM_DEV).transpose(1, 0, 2)
    elem_nodes = connect.reshape(4, devices, ELEM_DEV).transpose(1, 0, 2)
    mesh_lists = send_mesh.reshape(devices, GHOST_M)
    sub_lists = send_sub.reshape(devices, GHOST_S)
    picks_all = send_pick.reshape(STEPS, devices, SLOTS)
    lists_all = bucket_list.reshape(STEPS, CAND, devices, bucket_count).transpose(0, 2, 1, 3)
    masks_all = pair_mask.reshape(STEPS, CAND, devices, NODE_DEV).transpose(0, 2, 1, 3).astype(jnp.float32)
    slot_ids = jnp.arange(SLOTS, dtype=jnp.int32)
    block_ids = jnp.arange(block_count, dtype=jnp.int32)
    take_cols = jax.vmap(lambda source, column_ids: source[:, column_ids])
    take_rows = jax.vmap(lambda source, row_ids: source[row_ids])
    add_cols = jax.vmap(lambda target, column_ids, extra_force: target.at[:, column_ids].add(extra_force))
    scatter_cols = jax.vmap(lambda forces_in, column_ids: jnp.zeros((3, total_nodes), jnp.float32).at[:, column_ids].add(forces_in))

    def one_device(device_items):
        own_pos, slot_geo, cand_lists, live_mask = device_items
        slave_rows = own_pos.reshape(3, bucket_count, SEG).transpose(1, 0, 2)
        slave_force, reaction = contact_tiles(slave_rows, slot_geo[cand_lists], live_mask.reshape(CAND, bucket_count, SEG))
        onehot = (cand_lists.reshape(-1)[:, None] == slot_ids[None, :]).astype(jnp.float32)
        slot_react = jnp.dot(onehot.T, reaction.reshape(CAND * bucket_count, 3 * SEG), precision=HIGH)
        return (slave_force.transpose(1, 0, 2).reshape(3, NODE_DEV), slot_react.reshape(SLOTS, 3, SEG))
    for step_index in range(STEPS):
        packed = jnp.concatenate([positions, velocity], axis=1)
        from_mesh = roll_devices(take_cols(packed, mesh_lists), 1, 0)
        from_sub = roll_devices(take_cols(packed, sub_lists), 1, 1)
        pos_table = jnp.concatenate([positions, from_mesh[:, 0:3], from_sub[:, 0:3]], axis=2)
        vel_table = jnp.concatenate([velocity, from_mesh[:, 3:6], from_sub[:, 3:6]], axis=2)
        corner = take_cols(pos_table, elem_nodes)
        corner_vel = take_cols(vel_table, elem_nodes)
        internal, stress_now, centre, normal = jax.vmap(shell_forces)(corner, corner_vel, stress_now)
        geometry_blocks = jnp.concatenate([centre, normal], axis=1).reshape(devices, 6, block_count, SEG).transpose(0, 2, 1, 3)
        outgoing = take_rows(geometry_blocks, picks_all[step_index])
        incoming = swap_peers(outgoing)
        slave_force, slot_react = lax.map(one_device, (positions, incoming, lists_all[step_index], masks_all[step_index]))
        returned = swap_peers(slot_react).reshape(devices, SLOTS, 3 * SEG)
        pick_hot = (picks_all[step_index][:, :, None] == block_ids[None, None, :]).astype(jnp.float32)
        seg_react = jnp.einsum('dqb,dqx->dbx', pick_hot, returned, precision=HIGH)
        seg_react = seg_react.reshape(devices, block_count, 3, SEG).transpose(0, 2, 1, 3).reshape(devices, 3, ELEM_DEV)
        elem_force = 0.25 * seg_react[:, :, None, :] - internal
        node_force = scatter_cols(elem_force, elem_nodes)
        back_mesh = roll_devices(node_force[:, :, NODE_DEV:NODE_DEV + GHOST_M], -1, 0)
        back_sub = roll_devices(node_force[:, :, NODE_DEV + GHOST_M:], -1, 1)
        own_force = add_cols(add_cols(node_force[:, :, :NODE_DEV], mesh_lists, back_mesh), sub_lists, back_sub)
        velocity = velocity + TIME_STEP * (own_force + slave_force) / masses[:, None, :]
        positions = positions + TIME_STEP * velocity
    return (velocity.transpose(1, 0, 2).reshape(3, devices * NODE_DEV), stress_now.transpose(1, 0, 2).reshape(3, devices * ELEM_DEV))
```

```python
import functools
import math

import jax
import jax.numpy as jnp
from jax import lax
from jax.experimental import pallas as pl
from jax.experimental.pallas import tpu as pltpu
from jax.sharding import PartitionSpec as P

SEG = 128
STEPS = 4
CAP = 2
TIME_STEP = 0.2
YOUNG = 1.0
POISSON = 0.3
HOURGLASS = 0.01
PENALTY = 0.2
REACH = 4.0
PLANE_STIFF = YOUNG / (1.0 - POISSON * POISSON)
SHEAR_STIFF = YOUNG / (2.0 * (1.0 + POISSON))
EXP2_SCALE = math.log2(math.e) / REACH
MESH = pl.DeviceIdType.MESH
F32 = jnp.float32
BF16 = jnp.bfloat16
NT = (((1,), (1,)), ((), ()))
GHOST_ROWS = 4


def dot_nt(lhs, rhs):
    return lax.dot_general(lhs, rhs, NT, preferred_element_type=F32)


def halves(value):
    top = value.astype(BF16)
    return top, (value - top.astype(F32)).astype(BF16)


def cross(u, v):
    return (
        u[1] * v[2] - u[2] * v[1],
        u[2] * v[0] - u[0] * v[2],
        u[0] * v[1] - u[1] * v[0],
    )


def dot3(u, v):
    return u[0] * v[0] + u[1] * v[1] + u[2] * v[2]


def kernel(
    own_rows,
    blocks,
    cands,
    coords,
    veloc,
    mass_in,
    stress_in,
    connect,
    send_mesh,
    send_sub,
    picks,
    buckets,
    pick_lanes,
    bucket_lanes,
    pair_mask,
    vel_out,
    stress_out,
    ids,
    sids,
    pos,
    vel,
    mass,
    cpos,
    cvel,
    snow,
    nrm,
    area,
    geo,
    send_geo,
    recv_geo,
    onehot,
    onehot_back,
    spread,
    fint,
    table,
    pcol,
    mcol,
    wtop,
    wlow,
    wsum,
    slave,
    ret_send,
    ret_recv,
    p_send_m,
    p_send_s,
    p_recv_m,
    p_recv_s,
    v_send_m,
    v_send_s,
    v_recv_m,
    v_recv_s,
    f_send_m,
    f_send_s,
    f_recv_m,
    f_recv_s,
    halo_sem,
    geo_sem,
    ret_sem,
):
    peers = lax.axis_size("mesh")
    subs = lax.axis_size("sub")
    me = lax.axis_index("mesh")
    my_sub = lax.axis_index("sub")
    mesh_next = (lax.rem(me + 1, peers), my_sub)
    mesh_prev = (lax.rem(me + peers - 1, peers), my_sub)
    sub_next = (me, lax.rem(my_sub + 1, subs))
    sub_prev = (me, lax.rem(my_sub + subs - 1, subs))
    slots = peers * CAP
    chunks = blocks // 8
    pairs = cands * own_rows

    barrier = pltpu.get_barrier_semaphore()

    def greet(hop, carry):
        pl.semaphore_signal(
            barrier, inc=1, device_id=(lax.rem(me + hop, peers), my_sub), device_id_type=MESH
        )
        return carry

    lax.fori_loop(1, peers, greet, 0)
    for other in (sub_next, sub_prev):
        pl.semaphore_signal(barrier, inc=1, device_id=other, device_id_type=MESH)

    def lanes_of(row):
        return pl.ds(pl.multiple_of(row * SEG, SEG), SEG)

    def rows_of_nodes(row, carry):
        for c in range(3):
            pos[c, pl.ds(row, 1), :] = coords[pl.ds(c, 1), lanes_of(row)]
            vel[c, pl.ds(row, 1), :] = veloc[pl.ds(c, 1), lanes_of(row)]
        mass[pl.ds(row, 1), :] = mass_in[:, lanes_of(row)]
        return carry

    def rows_of_elems(row, carry):
        for c in range(3):
            snow[c, pl.ds(row, 1), :] = stress_in[pl.ds(c, 1), lanes_of(row)]
        for i in range(4):
            ids[i, pl.ds(row, 1), :] = connect[pl.ds(i, 1), lanes_of(row)]
        return carry

    lax.fori_loop(0, own_rows, rows_of_nodes, 0)
    for r in range(GHOST_ROWS):
        sids[r : r + 1, :] = send_mesh[:, r * SEG : (r + 1) * SEG]
        sids[GHOST_ROWS + r : GHOST_ROWS + r + 1, :] = send_sub[:, r * SEG : (r + 1) * SEG]

    def take(tables, rows, index):
        low = lax.bitwise_and(index, SEG - 1)
        high = lax.shift_right_logical(index, 7)
        found = [jnp.zeros(index.shape, F32) for _ in range(3)]
        for r in range(rows):
            here = high == r
            for c in range(3):
                source = jnp.broadcast_to(tables[c, r : r + 1, :], index.shape)
                got = jnp.take_along_axis(source, low, axis=1, mode="promise_in_bounds")
                found[c] = jnp.where(here, got, found[c])
        return found

    def halo_copy(src, dst, slot, target):
        return pltpu.make_async_remote_copy(
            src_ref=src,
            dst_ref=dst,
            send_sem=halo_sem.at[slot],
            recv_sem=halo_sem.at[slot + 1],
            device_id=target,
            device_id_type=MESH,
        )

    def velocity_copies(step):
        base = 4 + step * 8
        return (
            halo_copy(v_send_m.at[step], v_recv_m.at[step], base, mesh_next),
            halo_copy(v_send_s.at[step], v_recv_s.at[step], base + 2, sub_next),
        )

    def force_copies(step):
        base = 4 + step * 8 + 4
        return (
            halo_copy(f_send_m.at[step], f_recv_m.at[step], base, mesh_prev),
            halo_copy(f_send_s.at[step], f_recv_s.at[step], base + 2, sub_prev),
        )

    position_copies = (
        halo_copy(p_send_m, p_recv_m, 0, mesh_next),
        halo_copy(p_send_s, p_recv_s, 2, sub_next),
    )

    def stage_velocity(step):
        got = take(vel, own_rows, sids[...])
        for c in range(3):
            v_send_m[step, c] = got[c][:GHOST_ROWS]
            v_send_s[step, c] = got[c][GHOST_ROWS:]

    got = take(pos, own_rows, sids[...])
    for c in range(3):
        p_send_m[c] = got[c][:GHOST_ROWS]
        p_send_s[c] = got[c][GHOST_ROWS:]
    stage_velocity(0)

    pl.semaphore_wait(barrier, peers + 1)
    for copy in position_copies + velocity_copies(0):
        copy.start()

    lax.fori_loop(0, blocks, rows_of_elems, 0)

    def make_onehot(row, carry):
        lane = lax.broadcasted_iota(jnp.int32, (2 * SEG, SEG), 0)
        for i in range(4):
            index = ids[i, pl.ds(row, 1), :]
            low = lax.bitwise_and(index, SEG - 1)
            low = jnp.where(index >= own_rows * SEG, low + SEG, low)
            hot = jnp.where(lane == low, 1.0, 0.0).astype(BF16)
            onehot[:, pl.ds(pl.multiple_of((row * 4 + i) * SEG, SEG), SEG)] = hot
        return carry

    lax.fori_loop(0, blocks, make_onehot, 0)
    for r in range(2 * GHOST_ROWS):
        lane = lax.broadcasted_iota(jnp.int32, (SEG, SEG), 0)
        low = lax.bitwise_and(sids[r : r + 1, :], SEG - 1)
        onehot_back[:, r * SEG : (r + 1) * SEG] = jnp.where(lane == low, 1.0, 0.0).astype(BF16)

    for copy in position_copies:
        copy.wait()
    for c in range(3):
        table[c, :own_rows, :] = pos[c]
        table[c, own_rows : own_rows + GHOST_ROWS, :] = p_recv_m[c]
        table[c, own_rows + GHOST_ROWS :, :] = p_recv_s[c]

    def first_positions(part, carry):
        rows = pl.ds(pl.multiple_of(part * 8, 8), 8)
        for i in range(4):
            got = take(table, own_rows + 2 * GHOST_ROWS, ids[i, rows, :])
            for c in range(3):
                cpos[i, c, rows, :] = got[c]
        return carry

    lax.fori_loop(0, chunks, first_positions, 0)

    high_lane = lax.broadcasted_iota(jnp.int32, (16, SEG), 0)

    def scatter(value_of):
        def one_row(row, carry):
            for i in range(4):
                index = ids[i, pl.ds(row, 1), :]
                high = lax.bitwise_and(lax.shift_right_logical(index, 7), 15)
                here = high_lane == high
                at = pl.ds(pl.multiple_of(i * SEG, SEG), SEG)
                for c in range(3):
                    top, low = halves(jnp.where(here, value_of(i, c, row), 0.0))
                    spread[c * 32 : c * 32 + 16, at] = top
                    spread[c * 32 + 16 : c * 32 + 32, at] = low
            cols = pl.ds(pl.multiple_of(row * 4 * SEG, SEG), 4 * SEG)
            return carry + dot_nt(spread[...], onehot[:, cols])

        total = lax.fori_loop(0, blocks, one_row, jnp.zeros((96, 2 * SEG), F32))
        return [total[c * 32 : c * 32 + 16] + total[c * 32 + 16 : c * 32 + 32] for c in range(3)]

    def one_step(step, step_carry):
        for copy in velocity_copies(step):
            copy.wait()
        for c in range(3):
            vel[c, own_rows : own_rows + GHOST_ROWS, :] = v_recv_m[step, c]
            vel[c, own_rows + GHOST_ROWS :, :] = v_recv_s[step, c]
        advance = jnp.where(step > 0, TIME_STEP, 0.0).astype(F32)

        def shapes(part, carry):
            rows = pl.ds(pl.multiple_of(part * 8, 8), 8)
            a = []
            for i in range(4):
                w = take(vel, own_rows + 2 * GHOST_ROWS, ids[i, rows, :])
                at = []
                for c in range(3):
                    cvel[i, c, rows, :] = w[c]
                    moved = cpos[i, c, rows, :] + advance * w[c]
                    cpos[i, c, rows, :] = moved
                    at.append(moved)
                a.append(at)
            raw = cross(
                [a[2][c] - a[0][c] for c in range(3)], [a[3][c] - a[1][c] for c in range(3)]
            )
            twice = jnp.maximum(jnp.sqrt(dot3(raw, raw)), 1.0)
            area[rows, :] = twice
            for c in range(3):
                n = raw[c] / twice
                centre = 0.25 * (a[0][c] + a[1][c] + a[2][c] + a[3][c])
                nrm[c, rows, :] = n
                geo[rows, c, :] = centre
                geo[rows, 3 + c, :] = n
            return carry

        lax.fori_loop(0, chunks, shapes, 0)

        def block_copy(peer):
            return pltpu.make_async_remote_copy(
                src_ref=send_geo.at[pl.ds(peer * CAP, CAP)],
                dst_ref=recv_geo.at[step, pl.ds(me * CAP, CAP)],
                send_sem=geo_sem.at[0, step],
                recv_sem=geo_sem.at[1, step],
                device_id=(peer, my_sub),
                device_id_type=MESH,
            )

        def send_blocks(hop, carry):
            peer = lax.rem(me + hop, peers)
            for c in range(CAP):
                send_geo[peer * CAP + c] = geo[picks[step, peer * CAP + c]]
            block_copy(peer).start()
            return carry

        lax.fori_loop(1, peers, send_blocks, 0)
        for c in range(CAP):
            recv_geo[step, me * CAP + c] = geo[picks[step, me * CAP + c]]

        def inner_forces(part, carry):
            rows = pl.ds(pl.multiple_of(part * 8, 8), 8)
            a = [[cpos[i, c, rows, :] for c in range(3)] for i in range(4)]
            w = [[cvel[i, c, rows, :] for c in range(3)] for i in range(4)]
            n = [nrm[c, rows, :] for c in range(3)]
            twice = area[rows, :]
            centre = [geo[rows, c, :] for c in range(3)]
            side = [a[1][c] - a[0][c] for c in range(3)]
            length = jnp.maximum(jnp.sqrt(dot3(side, side)), 1.0)
            one = [side[c] / length for c in range(3)]
            two = cross(n, one)
            rel = [[a[i][c] - centre[c] for c in range(3)] for i in range(4)]
            x = [dot3(rel[i], one) for i in range(4)]
            y = [dot3(rel[i], two) for i in range(4)]
            u = [dot3(w[i], one) for i in range(4)]
            v = [dot3(w[i], two) for i in range(4)]
            inverse = 1.0 / twice
            b20, b31 = (y[2] - y[0]) * inverse, (y[1] - y[3]) * inverse
            bx = [b31, b20, -b31, -b20]
            c02, c31 = (x[0] - x[2]) * inverse, (x[3] - x[1]) * inverse
            by = [c31, c02, -c31, -c02]
            exx = b31 * (u[0] - u[2]) + b20 * (u[1] - u[3])
            eyy = c31 * (v[0] - v[2]) + c02 * (v[1] - v[3])
            exy = (
                c31 * (u[0] - u[2]) + c02 * (u[1] - u[3]) + b31 * (v[0] - v[2]) + b20 * (v[1] - v[3])
            )
            s0 = snow[0, rows, :] + TIME_STEP * (PLANE_STIFF * (exx + POISSON * eyy))
            s1 = snow[1, rows, :] + TIME_STEP * (PLANE_STIFF * (POISSON * exx + eyy))
            s2 = snow[2, rows, :] + TIME_STEP * (SHEAR_STIFF * exy)
            snow[0, rows, :] = s0
            snow[1, rows, :] = s1
            snow[2, rows, :] = s2
            half = 0.5 * twice
            hx = x[0] - x[1] + x[2] - x[3]
            hy = y[0] - y[1] + y[2] - y[3]
            signs = (1.0, -1.0, 1.0, -1.0)
            g = [signs[i] - hx * bx[i] - hy * by[i] for i in range(4)]
            r = [
                HOURGLASS * (g[0] * w[0][c] + g[1] * w[1][c] + g[2] * w[2][c] + g[3] * w[3][c])
                for c in range(3)
            ]
            for i in range(4):
                fx = half * (bx[i] * s0 + by[i] * s2)
                fy = half * (by[i] * s1 + bx[i] * s2)
                for c in range(3):
                    fint[i, c, rows, :] = -(fx * one[c] + fy * two[c] + g[i] * r[c])
            return carry

        lax.fori_loop(0, chunks, inner_forces, 0)
        node_force = scatter(lambda i, c, row: fint[i, c, pl.ds(row, 1), :])

        def columns(j, carry):
            for c in range(3):
                row = jnp.broadcast_to(pos[c, pl.ds(j, 1), :], (SEG, SEG))
                pcol[c, j] = jnp.transpose(row)
            for k in range(cands):
                row = pair_mask[step, pl.ds(k, 1), lanes_of(j)].astype(F32) * PENALTY
                mcol[k, j] = jnp.transpose(jnp.broadcast_to(row, (SEG, SEG)))
            return carry

        lax.fori_loop(0, own_rows, columns, 0)

        slot_row = lax.broadcasted_iota(jnp.int32, (slots, pairs * 8), 0)
        slot_row = jnp.where(slot_row < peers, slot_row * CAP, (slot_row - peers) * CAP + 1)
        slot_hot = jnp.where(slot_row == bucket_lanes[pl.ds(step, 1), :], 1.0, 0.0).astype(BF16)

        everything = pl.ds(0, slots - CAP)
        whole = pltpu.make_async_remote_copy(
            src_ref=send_geo.at[everything],
            dst_ref=recv_geo.at[step, everything],
            send_sem=geo_sem.at[0, step],
            recv_sem=geo_sem.at[1, step],
            device_id=mesh_next,
            device_id_type=MESH,
        )
        whole.wait_recv()

        def contact(j, carry):
            normals = []
            for k in range(cands):
                block = recv_geo[step, buckets[step, k * own_rows + j]]
                rows = [jnp.broadcast_to(block[q : q + 1], (16, SEG)) for q in range(6)]
                down = [-rows[3 + c] for c in range(3)]
                normals.append(block[3:6])
                total = jnp.zeros((8, SEG), F32)
                for part in range(SEG // 16):
                    at = slice(part * 16, part * 16 + 16)
                    o = [pcol[c, j, at, :] - rows[c] for c in range(3)]
                    depth = dot3(o, down)
                    reach = depth * depth - dot3(o, o)
                    weight = (
                        jnp.maximum(depth, 0.0) * jnp.exp2(reach * EXP2_SCALE) * mcol[k, j, at, :]
                    )
                    total = total + weight[:8] + weight[8:]
                    top, low = halves(weight)
                    wtop[at, k * SEG : (k + 1) * SEG] = top
                    wlow[at, k * SEG : (k + 1) * SEG] = low
                wsum[pl.ds(pl.multiple_of((k * own_rows + j) * 8, 8), 8), :] = total
            zeros = jnp.zeros((5, cands * SEG), F32)
            flat = jnp.concatenate([jnp.concatenate(normals, axis=1), zeros], axis=0)
            top, low = halves(flat)
            both = jnp.concatenate([top.astype(F32), low.astype(F32)], axis=0).astype(BF16)
            force = dot_nt(both, wtop[...])
            rest = dot_nt(both, wlow[...])
            force = force[:8] + force[8:] + rest[:8]
            for c in range(3):
                slave[c, pl.ds(j, 1), :] = force[c : c + 1]
            return carry

        lax.fori_loop(0, own_rows, contact, 0)

        top, low = halves(wsum[...])
        slot_sum = jnp.dot(slot_hot, top, preferred_element_type=F32) + jnp.dot(
            slot_hot, low, preferred_element_type=F32
        )
        for c in range(CAP):
            ret_send[step, :, c, :] = slot_sum[c * peers : (c + 1) * peers]

        def return_copy(peer):
            return pltpu.make_async_remote_copy(
                src_ref=ret_send.at[step, peer],
                dst_ref=ret_recv.at[step, me],
                send_sem=ret_sem.at[0, step],
                recv_sem=ret_sem.at[1, step],
                device_id=(peer, my_sub),
                device_id_type=MESH,
            )

        def send_back(hop, carry):
            return_copy(lax.rem(me + hop, peers)).start()
            return carry

        lax.fori_loop(1, peers, send_back, 0)
        ret_recv[step, me] = ret_send[step, me]
        pick_hot = lax.broadcasted_iota(jnp.int32, (blocks, slots), 0)
        pick_hot = jnp.where(pick_hot == pick_lanes[pl.ds(step, 1), :], 1.0, 0.0).astype(BF16)
        others = pl.ds(0, peers - 1)
        back = pltpu.make_async_remote_copy(
            src_ref=ret_send.at[step, others],
            dst_ref=ret_recv.at[step, others],
            send_sem=ret_sem.at[0, step],
            recv_sem=ret_sem.at[1, step],
            device_id=mesh_next,
            device_id_type=MESH,
        )
        back.wait_recv()
        returned = jnp.concatenate([ret_recv[step, :, c, :] for c in range(CAP)], axis=0)
        top, low = halves(returned)
        press = jnp.dot(pick_hot, top, preferred_element_type=F32) + jnp.dot(
            pick_hot, low, preferred_element_type=F32
        )
        for c in range(3):
            fint[0, c] = -0.25 * nrm[c] * press
        react = scatter(lambda i, c, row: fint[0, c, pl.ds(row, 1), :])
        force = [node_force[c] + react[c] for c in range(3)]
        for c in range(3):
            f_send_m[step, c] = force[c][:GHOST_ROWS, SEG:]
            f_send_s[step, c] = force[c][GHOST_ROWS : 2 * GHOST_ROWS, SEG:]
        back_copies = force_copies(step)
        for copy in back_copies:
            copy.start()
        for copy in back_copies:
            copy.wait()
        terms = []
        for c in range(3):
            came = jnp.concatenate([f_recv_m[step, c], f_recv_s[step, c]], axis=0)
            tops, lows = [], []
            for r in range(2 * GHOST_ROWS):
                high = lax.shift_right_logical(sids[r : r + 1, :], 7)
                top, low = halves(jnp.where(high_lane == high, came[r : r + 1], 0.0))
                tops.append(top)
                lows.append(low)
            terms.append(jnp.concatenate(tops, axis=1))
            terms.append(jnp.concatenate(lows, axis=1))
        added = dot_nt(jnp.concatenate(terms, axis=0), onehot_back[...])
        for c in range(3):
            own = force[c][:own_rows, :SEG]
            own = own + added[c * 32 : c * 32 + own_rows] + added[c * 32 + 16 : c * 32 + 16 + own_rows]
            now = vel[c, :own_rows, :] + TIME_STEP * (own + slave[c]) / mass[...]
            vel[c, :own_rows, :] = now
            pos[c] = pos[c] + TIME_STEP * now
        whole.wait_send()
        back.wait_send()

        @pl.when(step < STEPS - 1)
        def _():
            stage_velocity(step + 1)
            for copy in velocity_copies(step + 1):
                copy.start()

        return step_carry

    lax.fori_loop(0, STEPS, one_step, 0)
    vel_out[...] = vel[:, :own_rows, :]
    stress_out[...] = snow[...]


def per_device(
    coords, veloc, node_mass, stress, connect, send_mesh, send_sub, send_pick, bucket_list, pair_mask
):
    peers = lax.axis_size("mesh")
    nodes = coords.shape[1]
    elems = stress.shape[1]
    own_rows, blocks = nodes // SEG, elems // SEG
    cands = bucket_list.shape[1]
    slots = send_pick.shape[1]
    pairs = cands * own_rows
    flat_list = bucket_list.reshape(STEPS, pairs)
    bucket_lanes = jnp.repeat(flat_list, 8, axis=1)
    pick_lanes = send_pick.reshape(STEPS, peers, CAP).transpose(0, 2, 1).reshape(STEPS, slots)
    table_rows = own_rows + 2 * GHOST_ROWS
    ghost = (3, GHOST_ROWS, SEG)
    in_vmem = pl.BlockSpec(memory_space=pltpu.VMEM)
    in_smem = pl.BlockSpec(memory_space=pltpu.SMEM)
    v = pltpu.VMEM
    vel_rows, stress_rows = pl.pallas_call(
        functools.partial(kernel, own_rows, blocks, cands),
        out_shape=(
            jax.ShapeDtypeStruct((3, own_rows, SEG), F32),
            jax.ShapeDtypeStruct((3, blocks, SEG), F32),
        ),
        in_specs=[in_vmem] * 7 + [in_smem] * 2 + [in_vmem] * 3,
        out_specs=(in_vmem, in_vmem),
        scratch_shapes=[
            v((4, blocks, SEG), jnp.int32),
            v((2 * GHOST_ROWS, SEG), jnp.int32),
            v((3, own_rows, SEG), F32),
            v((3, table_rows, SEG), F32),
            v((own_rows, SEG), F32),
            v((4, 3, blocks, SEG), F32),
            v((4, 3, blocks, SEG), F32),
            v((3, blocks, SEG), F32),
            v((3, blocks, SEG), F32),
            v((blocks, SEG), F32),
            v((blocks, 6, SEG), F32),
            v((slots, 6, SEG), F32),
            v((STEPS, slots, 6, SEG), F32),
            v((2 * SEG, 4 * elems), BF16),
            v((SEG, 2 * GHOST_ROWS * SEG), BF16),
            v((96, 4 * SEG), BF16),
            v((4, 3, blocks, SEG), F32),
            v((3, table_rows, SEG), F32),
            v((3, own_rows, SEG, SEG), F32),
            v((cands, own_rows, SEG, SEG), F32),
            v((SEG, cands * SEG), BF16),
            v((SEG, cands * SEG), BF16),
            v((pairs * 8, SEG), F32),
            v((3, own_rows, SEG), F32),
            v((STEPS, peers, CAP, SEG), F32),
            v((STEPS, peers, CAP, SEG), F32),
            v(ghost, F32),
            v(ghost, F32),
            v(ghost, F32),
            v(ghost, F32),
            v((STEPS,) + ghost, F32),
            v((STEPS,) + ghost, F32),
            v((STEPS,) + ghost, F32),
            v((STEPS,) + ghost, F32),
            v((STEPS,) + ghost, F32),
            v((STEPS,) + ghost, F32),
            v((STEPS,) + ghost, F32),
            v((STEPS,) + ghost, F32),
            pltpu.SemaphoreType.DMA((4 + STEPS * 8,)),
            pltpu.SemaphoreType.DMA((2, STEPS)),
            pltpu.SemaphoreType.DMA((2, STEPS)),
        ],
        compiler_params=pltpu.CompilerParams(
            collective_id=0, has_side_effects=True, vmem_limit_bytes=56 * 1024 * 1024
        ),
    )(
        coords,
        veloc,
        node_mass.reshape(1, nodes),
        stress,
        connect,
        send_mesh.reshape(1, -1),
        send_sub.reshape(1, -1),
        send_pick,
        flat_list,
        pick_lanes,
        bucket_lanes,
        pair_mask,
    )
    return vel_rows.reshape(3, nodes), stress_rows.reshape(3, elems)


def solution(mesh):
    both = ("mesh", "sub")
    return jax.shard_map(
        per_device,
        mesh=mesh,
        in_specs=(
            P(None, both),
            P(None, both),
            P(both),
            P(None, both),
            P(None, both),
            P(both),
            P(both),
            P(None, both),
            P(None, None, both),
            P(None, None, both),
        ),
        out_specs=(P(None, both), P(None, both)),
        check_vma=False,
    )
```

```python
import functools
import math

import jax
import jax.numpy as jnp
from jax import lax
from jax.experimental import pallas as pl
from jax.experimental.pallas import tpu as pltpu
from jax.sharding import PartitionSpec as P

SEG = 128
STEPS = 4
CAP = 2
TIME_STEP = 0.2
YOUNG = 1.0
POISSON = 0.3
HOURGLASS = 0.01
PENALTY = 0.2
REACH = 4.0
PLANE_STIFF = YOUNG / (1.0 - POISSON * POISSON)
SHEAR_STIFF = YOUNG / (2.0 * (1.0 + POISSON))
EXP2_SCALE = math.log2(math.e) / REACH
MESH = pl.DeviceIdType.MESH
F32 = jnp.float32
BF16 = jnp.bfloat16
NT = (((1,), (1,)), ((), ()))
GHOST_ROWS = 4


def dot_nt(lhs, rhs):
    return lax.dot_general(lhs, rhs, NT, preferred_element_type=F32)


def halves(value):
    top = value.astype(BF16)
    return top, (value - top.astype(F32)).astype(BF16)


def cross(u, v):
    return (
        u[1] * v[2] - u[2] * v[1],
        u[2] * v[0] - u[0] * v[2],
        u[0] * v[1] - u[1] * v[0],
    )


def dot3(u, v):
    return u[0] * v[0] + u[1] * v[1] + u[2] * v[2]


def kernel(
    own_rows,
    blocks,
    cands,
    coords,
    veloc,
    mass_in,
    stress_in,
    connect,
    send_mesh,
    send_sub,
    picks,
    buckets,
    pick_lanes,
    bucket_lanes,
    pair_mask,
    vel_out,
    stress_out,
    ids,
    sids,
    pos,
    vel,
    mass,
    cpos,
    cvel,
    snow,
    nrm,
    area,
    geo,
    send_geo,
    recv_geo,
    onehot,
    onehot_back,
    rowhot,
    spread,
    ftop,
    flow,
    table,
    pcol,
    mcol,
    wtop_a,
    wlow_a,
    normals_a,
    wtop_b,
    wlow_b,
    normals_b,
    wsum,
    slave,
    ret_send,
    ret_recv,
    p_send_m,
    p_send_s,
    p_recv_m,
    p_recv_s,
    v_send_m,
    v_send_s,
    v_recv_m,
    v_recv_s,
    f_send_m,
    f_send_s,
    f_recv_m,
    f_recv_s,
    halo_sem,
    geo_sem,
    ret_sem,
):
    peers = lax.axis_size("mesh")
    subs = lax.axis_size("sub")
    me = lax.axis_index("mesh")
    my_sub = lax.axis_index("sub")
    mesh_next = (lax.rem(me + 1, peers), my_sub)
    mesh_prev = (lax.rem(me + peers - 1, peers), my_sub)
    sub_next = (me, lax.rem(my_sub + 1, subs))
    sub_prev = (me, lax.rem(my_sub + subs - 1, subs))
    slots = peers * CAP
    chunks = blocks // 8
    pairs = cands * own_rows

    barrier = pltpu.get_barrier_semaphore()

    def greet(hop, carry):
        pl.semaphore_signal(
            barrier, inc=1, device_id=(lax.rem(me + hop, peers), my_sub), device_id_type=MESH
        )
        return carry

    lax.fori_loop(1, peers, greet, 0)
    for other in (sub_next, sub_prev):
        pl.semaphore_signal(barrier, inc=1, device_id=other, device_id_type=MESH)

    def lanes_of(row):
        return pl.ds(pl.multiple_of(row * SEG, SEG), SEG)

    def rows_of_nodes(row, carry):
        for c in range(3):
            pos[c, pl.ds(row, 1), :] = coords[pl.ds(c, 1), lanes_of(row)]
            vel[c, pl.ds(row, 1), :] = veloc[pl.ds(c, 1), lanes_of(row)]
        mass[pl.ds(row, 1), :] = mass_in[:, lanes_of(row)]
        return carry

    def rows_of_elems(row, carry):
        for c in range(3):
            snow[c, pl.ds(row, 1), :] = stress_in[pl.ds(c, 1), lanes_of(row)]
        for i in range(4):
            ids[i, pl.ds(row, 1), :] = connect[pl.ds(i, 1), lanes_of(row)]
        return carry

    lax.fori_loop(0, own_rows, rows_of_nodes, 0)
    for r in range(GHOST_ROWS):
        sids[r : r + 1, :] = send_mesh[:, r * SEG : (r + 1) * SEG]
        sids[GHOST_ROWS + r : GHOST_ROWS + r + 1, :] = send_sub[:, r * SEG : (r + 1) * SEG]

    def take(tables, rows, index):
        low = lax.bitwise_and(index, SEG - 1)
        high = lax.shift_right_logical(index, 7)
        found = [jnp.zeros(index.shape, F32) for _ in range(3)]
        for r in range(rows):
            here = high == r
            for c in range(3):
                source = jnp.broadcast_to(tables[c, r : r + 1, :], index.shape)
                got = jnp.take_along_axis(source, low, axis=1, mode="promise_in_bounds")
                found[c] = jnp.where(here, got, found[c])
        return found

    def halo_copy(src, dst, slot, target):
        return pltpu.make_async_remote_copy(
            src_ref=src,
            dst_ref=dst,
            send_sem=halo_sem.at[slot],
            recv_sem=halo_sem.at[slot + 1],
            device_id=target,
            device_id_type=MESH,
        )

    def velocity_copies(step):
        base = 4 + step * 8
        return (
            halo_copy(v_send_m.at[step], v_recv_m.at[step], base, mesh_next),
            halo_copy(v_send_s.at[step], v_recv_s.at[step], base + 2, sub_next),
        )

    def force_copies(step):
        base = 4 + step * 8 + 4
        return (
            halo_copy(f_send_m.at[step], f_recv_m.at[step], base, mesh_prev),
            halo_copy(f_send_s.at[step], f_recv_s.at[step], base + 2, sub_prev),
        )

    position_copies = (
        halo_copy(p_send_m, p_recv_m, 0, mesh_next),
        halo_copy(p_send_s, p_recv_s, 2, sub_next),
    )

    def stage_velocity(step):
        got = take(vel, own_rows, sids[...])
        for c in range(3):
            v_send_m[step, c] = got[c][:GHOST_ROWS]
            v_send_s[step, c] = got[c][GHOST_ROWS:]

    got = take(pos, own_rows, sids[...])
    for c in range(3):
        p_send_m[c] = got[c][:GHOST_ROWS]
        p_send_s[c] = got[c][GHOST_ROWS:]
    stage_velocity(0)

    pl.semaphore_wait(barrier, peers + 1)
    for copy in position_copies + velocity_copies(0):
        copy.start()

    lax.fori_loop(0, blocks, rows_of_elems, 0)
    for ref in (wtop_b, wlow_b, normals_b):
        ref[...] = jnp.zeros(ref.shape, BF16)

    high_lane = lax.broadcasted_iota(jnp.int32, (16, SEG), 0)
    ghost_lane = lax.bitwise_and(high_lane, 7) + own_rows

    def make_onehot(row, carry):
        lane = lax.broadcasted_iota(jnp.int32, (SEG, SEG), 0)
        for i in range(4):
            index = ids[i, pl.ds(row, 1), :]
            low = lax.bitwise_and(index, SEG - 1)
            high = lax.shift_right_logical(index, 7)
            cols = pl.ds(pl.multiple_of((row * 4 + i) * SEG, SEG), SEG)
            onehot[:, cols] = jnp.where(lane == low, 1.0, 0.0).astype(BF16)
            rowhot[:16, cols] = jnp.where(high_lane == high, 1.0, 0.0).astype(BF16)
            rowhot[16:, cols] = jnp.where(ghost_lane == high, 1.0, 0.0).astype(BF16)
        return carry

    lax.fori_loop(0, blocks, make_onehot, 0)
    for r in range(2 * GHOST_ROWS):
        lane = lax.broadcasted_iota(jnp.int32, (SEG, SEG), 0)
        low = lax.bitwise_and(sids[r : r + 1, :], SEG - 1)
        onehot_back[:, r * SEG : (r + 1) * SEG] = jnp.where(lane == low, 1.0, 0.0).astype(BF16)

    for copy in position_copies:
        copy.wait()
    for c in range(3):
        table[c, :own_rows, :] = pos[c]
        table[c, own_rows : own_rows + GHOST_ROWS, :] = p_recv_m[c]
        table[c, own_rows + GHOST_ROWS :, :] = p_recv_s[c]

    def first_positions(part, carry):
        rows = pl.ds(pl.multiple_of(part * 8, 8), 8)
        for i in range(4):
            got = take(table, own_rows + 2 * GHOST_ROWS, ids[i, rows, :])
            for c in range(3):
                cpos[i, c, rows, :] = got[c]
        return carry

    lax.fori_loop(0, chunks, first_positions, 0)

    def scatter(corners):
        def one_part(part, carry):
            def one_row(r, inner):
                row = part * 8 + r
                values = []
                for i in range(corners):
                    for c in range(3):
                        top = ftop[i, c, pl.ds(row, 1), :]
                        low = flow[i, c, pl.ds(row, 1), :]
                        top8 = jnp.broadcast_to(top, (8, SEG))
                        low8 = jnp.broadcast_to(low, (8, SEG))
                        values.append(
                            (
                                jnp.concatenate([top8, top8], axis=0).astype(BF16),
                                jnp.concatenate([low8, low8], axis=0).astype(BF16),
                                jnp.concatenate([top8, low8], axis=0).astype(BF16),
                            )
                        )
                for i in range(4):
                    cols = pl.ds(pl.multiple_of((row * 4 + i) * SEG, SEG), SEG)
                    at = pl.ds(pl.multiple_of((r * 4 + i) * SEG, SEG), SEG)
                    here = rowhot[:16, cols]
                    away = rowhot[16:, cols]
                    for c in range(3):
                        top, low, both = values[(i if corners > 1 else 0) * 3 + c]
                        spread[c * 32 : c * 32 + 16, at] = here * top
                        spread[c * 32 + 16 : c * 32 + 32, at] = here * low
                        spread[96 + c * 16 : 112 + c * 16, at] = away * both
                return inner

            lax.fori_loop(0, 8, one_row, 0)
            cols = pl.ds(pl.multiple_of(part * 32 * SEG, 32 * SEG), 32 * SEG)
            return carry + dot_nt(spread[...], onehot[:, cols])

        total = lax.fori_loop(0, chunks, one_part, jnp.zeros((144, SEG), F32))
        own = [total[c * 32 : c * 32 + 16] + total[c * 32 + 16 : c * 32 + 32] for c in range(3)]
        ghost = [
            total[96 + c * 16 : 104 + c * 16] + total[104 + c * 16 : 112 + c * 16] for c in range(3)
        ]
        return own + ghost

    def store_halves(i, c, rows, value):
        top = value.astype(BF16).astype(F32)
        ftop[i, c, rows, :] = top
        flow[i, c, rows, :] = value - top

    def one_step(step, step_carry):
        for copy in velocity_copies(step):
            copy.wait()
        for c in range(3):
            vel[c, own_rows : own_rows + GHOST_ROWS, :] = v_recv_m[step, c]
            vel[c, own_rows + GHOST_ROWS :, :] = v_recv_s[step, c]
        advance = jnp.where(step > 0, TIME_STEP, 0.0).astype(F32)

        def shapes(part, carry):
            rows = pl.ds(pl.multiple_of(part * 8, 8), 8)
            a = []
            for i in range(4):
                w = take(vel, own_rows + 2 * GHOST_ROWS, ids[i, rows, :])
                at = []
                for c in range(3):
                    cvel[i, c, rows, :] = w[c]
                    moved = cpos[i, c, rows, :] + advance * w[c]
                    cpos[i, c, rows, :] = moved
                    at.append(moved)
                a.append(at)
            raw = cross(
                [a[2][c] - a[0][c] for c in range(3)], [a[3][c] - a[1][c] for c in range(3)]
            )
            twice = jnp.maximum(jnp.sqrt(dot3(raw, raw)), 1.0)
            area[rows, :] = twice
            for c in range(3):
                n = raw[c] / twice
                centre = 0.25 * (a[0][c] + a[1][c] + a[2][c] + a[3][c])
                nrm[c, rows, :] = n
                geo[rows, c, :] = centre
                geo[rows, 3 + c, :] = n
            return carry

        lax.fori_loop(0, chunks, shapes, 0)

        def block_copy(peer):
            return pltpu.make_async_remote_copy(
                src_ref=send_geo.at[pl.ds(peer * CAP, CAP)],
                dst_ref=recv_geo.at[step, pl.ds(me * CAP, CAP)],
                send_sem=geo_sem.at[0, step],
                recv_sem=geo_sem.at[1, step],
                device_id=(peer, my_sub),
                device_id_type=MESH,
            )

        def send_blocks(hop, carry):
            peer = lax.rem(me + hop, peers)
            for c in range(CAP):
                send_geo[peer * CAP + c] = geo[picks[step, peer * CAP + c]]
            block_copy(peer).start()
            return carry

        lax.fori_loop(1, peers, send_blocks, 0)
        for c in range(CAP):
            recv_geo[step, me * CAP + c] = geo[picks[step, me * CAP + c]]

        def inner_forces(part, carry):
            rows = pl.ds(pl.multiple_of(part * 8, 8), 8)
            a = [[cpos[i, c, rows, :] for c in range(3)] for i in range(4)]
            w = [[cvel[i, c, rows, :] for c in range(3)] for i in range(4)]
            n = [nrm[c, rows, :] for c in range(3)]
            twice = area[rows, :]
            centre = [geo[rows, c, :] for c in range(3)]
            side = [a[1][c] - a[0][c] for c in range(3)]
            length = jnp.maximum(jnp.sqrt(dot3(side, side)), 1.0)
            one = [side[c] / length for c in range(3)]
            two = cross(n, one)
            rel = [[a[i][c] - centre[c] for c in range(3)] for i in range(4)]
            x = [dot3(rel[i], one) for i in range(4)]
            y = [dot3(rel[i], two) for i in range(4)]
            u = [dot3(w[i], one) for i in range(4)]
            v = [dot3(w[i], two) for i in range(4)]
            inverse = 1.0 / twice
            b20, b31 = (y[2] - y[0]) * inverse, (y[1] - y[3]) * inverse
            bx = [b31, b20, -b31, -b20]
            c02, c31 = (x[0] - x[2]) * inverse, (x[3] - x[1]) * inverse
            by = [c31, c02, -c31, -c02]
            exx = b31 * (u[0] - u[2]) + b20 * (u[1] - u[3])
            eyy = c31 * (v[0] - v[2]) + c02 * (v[1] - v[3])
            exy = (
                c31 * (u[0] - u[2]) + c02 * (u[1] - u[3]) + b31 * (v[0] - v[2]) + b20 * (v[1] - v[3])
            )
            s0 = snow[0, rows, :] + TIME_STEP * (PLANE_STIFF * (exx + POISSON * eyy))
            s1 = snow[1, rows, :] + TIME_STEP * (PLANE_STIFF * (POISSON * exx + eyy))
            s2 = snow[2, rows, :] + TIME_STEP * (SHEAR_STIFF * exy)
            snow[0, rows, :] = s0
            snow[1, rows, :] = s1
            snow[2, rows, :] = s2
            half = 0.5 * twice
            hx = x[0] - x[1] + x[2] - x[3]
            hy = y[0] - y[1] + y[2] - y[3]
            signs = (1.0, -1.0, 1.0, -1.0)
            g = [signs[i] - hx * bx[i] - hy * by[i] for i in range(4)]
            r = [
                HOURGLASS * (g[0] * w[0][c] + g[1] * w[1][c] + g[2] * w[2][c] + g[3] * w[3][c])
                for c in range(3)
            ]
            for i in range(4):
                fx = half * (bx[i] * s0 + by[i] * s2)
                fy = half * (by[i] * s1 + bx[i] * s2)
                for c in range(3):
                    store_halves(i, c, rows, -(fx * one[c] + fy * two[c] + g[i] * r[c]))
            return carry

        lax.fori_loop(0, chunks, inner_forces, 0)
        node_force = scatter(4)

        def columns(j, carry):
            for c in range(3):
                row = jnp.broadcast_to(pos[c, pl.ds(j, 1), :], (SEG, SEG))
                pcol[c, j] = jnp.transpose(row)
            for k in range(cands):
                row = pair_mask[step, pl.ds(k, 1), lanes_of(j)].astype(F32) * PENALTY
                mcol[k, j] = jnp.transpose(jnp.broadcast_to(row, (SEG, SEG)))
            return carry

        lax.fori_loop(0, own_rows, columns, 0)

        slot_row = lax.broadcasted_iota(jnp.int32, (slots, pairs * 8), 0)
        slot_row = jnp.where(slot_row < peers, slot_row * CAP, (slot_row - peers) * CAP + 1)
        slot_hot = jnp.where(slot_row == bucket_lanes[pl.ds(step, 1), :], 1.0, 0.0).astype(BF16)

        everything = pl.ds(0, slots - CAP)
        whole = pltpu.make_async_remote_copy(
            src_ref=send_geo.at[everything],
            dst_ref=recv_geo.at[step, everything],
            send_sem=geo_sem.at[0, step],
            recv_sem=geo_sem.at[1, step],
            device_id=mesh_next,
            device_id_type=MESH,
        )
        whole.wait_recv()

        def contact(j, wtop, wlow, normals_at):
            normals = []
            for k in range(cands):
                block = recv_geo[step, buckets[step, k * own_rows + j]]
                rows = [jnp.broadcast_to(block[q : q + 1], (16, SEG)) for q in range(6)]
                down = [-rows[3 + c] for c in range(3)]
                normals.append(block[3:6])
                total = jnp.zeros((8, SEG), F32)
                for part in range(SEG // 16):
                    at = slice(part * 16, part * 16 + 16)
                    o = [pcol[c, j, at, :] - rows[c] for c in range(3)]
                    depth = dot3(o, down)
                    reach = depth * depth - dot3(o, o)
                    weight = (
                        jnp.maximum(depth, 0.0) * jnp.exp2(reach * EXP2_SCALE) * mcol[k, j, at, :]
                    )
                    total = total + weight[:8] + weight[8:]
                    top, low = halves(weight)
                    wtop[at, k * SEG : (k + 1) * SEG] = top
                    wlow[at, k * SEG : (k + 1) * SEG] = low
                wsum[pl.ds(pl.multiple_of((k * own_rows + j) * 8, 8), 8), :] = total
            zeros = jnp.zeros((5, cands * SEG), F32)
            flat = jnp.concatenate([jnp.concatenate(normals, axis=1), zeros], axis=0)
            top = flat.astype(BF16).astype(F32)
            normals_at[...] = jnp.concatenate([top, flat - top], axis=0).astype(BF16)

        def push(j, wtop, wlow, normals_at):
            both = normals_at[...]
            force = dot_nt(both, wtop[...])
            rest = dot_nt(both, wlow[...])
            force = force[:8] + force[8:] + rest[:8]
            for c in range(3):
                slave[c, pl.ds(j, 1), :] = force[c : c + 1]

        even = (wtop_a, wlow_a, normals_a)
        odd = (wtop_b, wlow_b, normals_b)

        def contact_pair(half, carry):
            push(jnp.maximum(2 * half - 1, 0), *odd)
            contact(2 * half, *even)
            push(2 * half, *even)
            contact(2 * half + 1, *odd)
            return carry

        lax.fori_loop(0, own_rows // 2, contact_pair, 0)
        push(own_rows - 1, *odd)

        top, low = halves(wsum[...])
        slot_sum = jnp.dot(slot_hot, top, preferred_element_type=F32) + jnp.dot(
            slot_hot, low, preferred_element_type=F32
        )
        for c in range(CAP):
            ret_send[step, :, c, :] = slot_sum[c * peers : (c + 1) * peers]

        def return_copy(peer):
            return pltpu.make_async_remote_copy(
                src_ref=ret_send.at[step, peer],
                dst_ref=ret_recv.at[step, me],
                send_sem=ret_sem.at[0, step],
                recv_sem=ret_sem.at[1, step],
                device_id=(peer, my_sub),
                device_id_type=MESH,
            )

        def send_back(hop, carry):
            return_copy(lax.rem(me + hop, peers)).start()
            return carry

        lax.fori_loop(1, peers, send_back, 0)
        ret_recv[step, me] = ret_send[step, me]
        pick_hot = lax.broadcasted_iota(jnp.int32, (blocks, slots), 0)
        pick_hot = jnp.where(pick_hot == pick_lanes[pl.ds(step, 1), :], 1.0, 0.0).astype(BF16)
        others = pl.ds(0, peers - 1)
        back = pltpu.make_async_remote_copy(
            src_ref=ret_send.at[step, others],
            dst_ref=ret_recv.at[step, others],
            send_sem=ret_sem.at[0, step],
            recv_sem=ret_sem.at[1, step],
            device_id=mesh_next,
            device_id_type=MESH,
        )
        back.wait_recv()
        returned = jnp.concatenate([ret_recv[step, :, c, :] for c in range(CAP)], axis=0)
        top, low = halves(returned)
        press = jnp.dot(pick_hot, top, preferred_element_type=F32) + jnp.dot(
            pick_hot, low, preferred_element_type=F32
        )
        for c in range(3):
            store_halves(0, c, slice(None), -0.25 * nrm[c] * press)
        react = scatter(1)
        force = [node_force[c] + react[c] for c in range(6)]
        for c in range(3):
            f_send_m[step, c] = force[3 + c][:GHOST_ROWS]
            f_send_s[step, c] = force[3 + c][GHOST_ROWS:]
        back_copies = force_copies(step)
        for copy in back_copies:
            copy.start()
        for copy in back_copies:
            copy.wait()
        terms = []
        for c in range(3):
            came = jnp.concatenate([f_recv_m[step, c], f_recv_s[step, c]], axis=0)
            tops, lows = [], []
            for r in range(2 * GHOST_ROWS):
                high = lax.shift_right_logical(sids[r : r + 1, :], 7)
                top, low = halves(jnp.where(high_lane == high, came[r : r + 1], 0.0))
                tops.append(top)
                lows.append(low)
            terms.append(jnp.concatenate(tops, axis=1))
            terms.append(jnp.concatenate(lows, axis=1))
        added = dot_nt(jnp.concatenate(terms, axis=0), onehot_back[...])
        for c in range(3):
            own = force[c]
            own = own + added[c * 32 : c * 32 + own_rows] + added[c * 32 + 16 : c * 32 + 16 + own_rows]
            now = vel[c, :own_rows, :] + TIME_STEP * (own + slave[c]) / mass[...]
            vel[c, :own_rows, :] = now
            pos[c] = pos[c] + TIME_STEP * now
        whole.wait_send()
        back.wait_send()

        @pl.when(step < STEPS - 1)
        def _():
            stage_velocity(step + 1)
            for copy in velocity_copies(step + 1):
                copy.start()

        return step_carry

    lax.fori_loop(0, STEPS, one_step, 0)
    vel_out[...] = vel[:, :own_rows, :]
    stress_out[...] = snow[...]


def per_device(
    coords, veloc, node_mass, stress, connect, send_mesh, send_sub, send_pick, bucket_list, pair_mask
):
    peers = lax.axis_size("mesh")
    nodes = coords.shape[1]
    elems = stress.shape[1]
    own_rows, blocks = nodes // SEG, elems // SEG
    cands = bucket_list.shape[1]
    slots = send_pick.shape[1]
    pairs = cands * own_rows
    flat_list = bucket_list.reshape(STEPS, pairs)
    bucket_lanes = jnp.repeat(flat_list, 8, axis=1)
    pick_lanes = send_pick.reshape(STEPS, peers, CAP).transpose(0, 2, 1).reshape(STEPS, slots)
    table_rows = own_rows + 2 * GHOST_ROWS
    ghost = (3, GHOST_ROWS, SEG)
    in_vmem = pl.BlockSpec(memory_space=pltpu.VMEM)
    in_smem = pl.BlockSpec(memory_space=pltpu.SMEM)
    v = pltpu.VMEM
    vel_rows, stress_rows = pl.pallas_call(
        functools.partial(kernel, own_rows, blocks, cands),
        out_shape=(
            jax.ShapeDtypeStruct((3, own_rows, SEG), F32),
            jax.ShapeDtypeStruct((3, blocks, SEG), F32),
        ),
        in_specs=[in_vmem] * 7 + [in_smem] * 2 + [in_vmem] * 3,
        out_specs=(in_vmem, in_vmem),
        scratch_shapes=[
            v((4, blocks, SEG), jnp.int32),
            v((2 * GHOST_ROWS, SEG), jnp.int32),
            v((3, own_rows, SEG), F32),
            v((3, table_rows, SEG), F32),
            v((own_rows, SEG), F32),
            v((4, 3, blocks, SEG), F32),
            v((4, 3, blocks, SEG), F32),
            v((3, blocks, SEG), F32),
            v((3, blocks, SEG), F32),
            v((blocks, SEG), F32),
            v((blocks, 6, SEG), F32),
            v((slots, 6, SEG), F32),
            v((STEPS, slots, 6, SEG), F32),
            v((SEG, 4 * elems), BF16),
            v((SEG, 2 * GHOST_ROWS * SEG), BF16),
            v((32, 4 * elems), BF16),
            v((144, 32 * SEG), BF16),
            v((4, 3, blocks, SEG), F32),
            v((4, 3, blocks, SEG), F32),
            v((3, table_rows, SEG), F32),
            v((3, own_rows, SEG, SEG), F32),
            v((cands, own_rows, SEG, SEG), F32),
            v((SEG, cands * SEG), BF16),
            v((SEG, cands * SEG), BF16),
            v((16, cands * SEG), BF16),
            v((SEG, cands * SEG), BF16),
            v((SEG, cands * SEG), BF16),
            v((16, cands * SEG), BF16),
            v((pairs * 8, SEG), F32),
            v((3, own_rows, SEG), F32),
            v((STEPS, peers, CAP, SEG), F32),
            v((STEPS, peers, CAP, SEG), F32),
            v(ghost, F32),
            v(ghost, F32),
            v(ghost, F32),
            v(ghost, F32),
            v((STEPS,) + ghost, F32),
            v((STEPS,) + ghost, F32),
            v((STEPS,) + ghost, F32),
            v((STEPS,) + ghost, F32),
            v((STEPS,) + ghost, F32),
            v((STEPS,) + ghost, F32),
            v((STEPS,) + ghost, F32),
            v((STEPS,) + ghost, F32),
            pltpu.SemaphoreType.DMA((4 + STEPS * 8,)),
            pltpu.SemaphoreType.DMA((2, STEPS)),
            pltpu.SemaphoreType.DMA((2, STEPS)),
        ],
        compiler_params=pltpu.CompilerParams(
            collective_id=0, has_side_effects=True, vmem_limit_bytes=56 * 1024 * 1024
        ),
    )(
        coords,
        veloc,
        node_mass.reshape(1, nodes),
        stress,
        connect,
        send_mesh.reshape(1, -1),
        send_sub.reshape(1, -1),
        send_pick,
        flat_list,
        pick_lanes,
        bucket_lanes,
        pair_mask,
    )
    return vel_rows.reshape(3, nodes), stress_rows.reshape(3, elems)


def solution(mesh):
    both = ("mesh", "sub")
    return jax.shard_map(
        per_device,
        mesh=mesh,
        in_specs=(
            P(None, both),
            P(None, both),
            P(both),
            P(None, both),
            P(None, both),
            P(both),
            P(both),
            P(None, both),
            P(None, None, both),
            P(None, None, both),
        ),
        out_specs=(P(None, both), P(None, both)),
        check_vma=False,
    )
```

```python
import functools
import math

import jax
import jax.numpy as jnp
from jax import lax
from jax.experimental import pallas as pl
from jax.experimental.pallas import tpu as pltpu
from jax.sharding import PartitionSpec as P

SEG = 128
STEPS = 4
CAP = 2
TIME_STEP = 0.2
YOUNG = 1.0
POISSON = 0.3
HOURGLASS = 0.01
PENALTY = 0.2
REACH = 4.0
PLANE_STIFF = YOUNG / (1.0 - POISSON * POISSON)
SHEAR_STIFF = YOUNG / (2.0 * (1.0 + POISSON))
EXP2_SCALE = math.log2(math.e) / REACH
MESH = pl.DeviceIdType.MESH
F32 = jnp.float32
BF16 = jnp.bfloat16
NT = (((1,), (1,)), ((), ()))
GHOST_ROWS = 4


def dot_nt(lhs, rhs):
    return lax.dot_general(lhs, rhs, NT, preferred_element_type=F32)


def halves(value):
    top = value.astype(BF16)
    return top, (value - top.astype(F32)).astype(BF16)


def cross(u, v):
    return (
        u[1] * v[2] - u[2] * v[1],
        u[2] * v[0] - u[0] * v[2],
        u[0] * v[1] - u[1] * v[0],
    )


def dot3(u, v):
    return u[0] * v[0] + u[1] * v[1] + u[2] * v[2]


def kernel(
    own_rows,
    blocks,
    cands,
    coords,
    veloc,
    mass_in,
    stress_in,
    connect,
    send_mesh,
    send_sub,
    picks,
    buckets,
    pick_rows,
    pair_mask,
    vel_out,
    stress_out,
    ids,
    sids,
    pos,
    vel,
    mass,
    cpos,
    cvel,
    snow,
    nrm,
    area,
    geo,
    send_geo,
    recv_geo,
    onehot,
    onehot_back,
    rowhot,
    spread,
    ftop,
    flow,
    table,
    pcol,
    mcol,
    wtop_a,
    wlow_a,
    normals_a,
    wtop_b,
    wlow_b,
    normals_b,
    wsum,
    named,
    slave,
    ret_send,
    ret_recv,
    p_send_m,
    p_send_s,
    p_recv_m,
    p_recv_s,
    v_send_m,
    v_send_s,
    v_recv_m,
    v_recv_s,
    f_send_m,
    f_send_s,
    f_recv_m,
    f_recv_s,
    halo_sem,
    geo_sem,
    ret_sem,
):
    peers = lax.axis_size("mesh")
    subs = lax.axis_size("sub")
    me = lax.axis_index("mesh")
    my_sub = lax.axis_index("sub")
    mesh_next = (lax.rem(me + 1, peers), my_sub)
    mesh_prev = (lax.rem(me + peers - 1, peers), my_sub)
    sub_next = (me, lax.rem(my_sub + 1, subs))
    sub_prev = (me, lax.rem(my_sub + subs - 1, subs))
    slots = peers * CAP
    chunks = blocks // 8
    pairs = cands * own_rows

    ring_x, ring_z = 4, peers // 8
    my_core, my_z, my_x = me % 2, me // 2 % ring_z, me // (2 * ring_z)

    def spread_out(ring, turn):
        return ring // 2 + (turn + 1) // 2 * (1 - 2 * (turn % 2))

    def each_partner(act):
        def one_z(turn, carry):
            z = lax.rem(my_z + spread_out(ring_z, turn), ring_z)
            for turn_x in range(ring_x):
                x = lax.rem(my_x + spread_out(ring_x, turn_x), ring_x)
                chip = (x * ring_z + z) * 2
                act(chip + 1 - my_core)
                if turn_x < ring_x - 1:
                    act(chip + my_core)
                else:
                    pl.when(turn < ring_z - 1)(lambda chip=chip: act(chip + my_core))
            return carry

        lax.fori_loop(0, ring_z, one_z, 0)

    barrier = pltpu.get_barrier_semaphore()

    def greet(hop, carry):
        pl.semaphore_signal(
            barrier, inc=1, device_id=(lax.rem(me + hop, peers), my_sub), device_id_type=MESH
        )
        return carry

    lax.fori_loop(1, peers, greet, 0)
    for other in (sub_next, sub_prev):
        pl.semaphore_signal(barrier, inc=1, device_id=other, device_id_type=MESH)

    def lanes_of(row):
        return pl.ds(pl.multiple_of(row * SEG, SEG), SEG)

    def rows_of_nodes(row, carry):
        for c in range(3):
            pos[c, pl.ds(row, 1), :] = coords[pl.ds(c, 1), lanes_of(row)]
            vel[c, pl.ds(row, 1), :] = veloc[pl.ds(c, 1), lanes_of(row)]
        mass[pl.ds(row, 1), :] = mass_in[:, lanes_of(row)]
        return carry

    def rows_of_elems(row, carry):
        for c in range(3):
            snow[c, pl.ds(row, 1), :] = stress_in[pl.ds(c, 1), lanes_of(row)]
        for i in range(4):
            ids[i, pl.ds(row, 1), :] = connect[pl.ds(i, 1), lanes_of(row)]
        return carry

    lax.fori_loop(0, own_rows, rows_of_nodes, 0)
    for r in range(GHOST_ROWS):
        sids[r : r + 1, :] = send_mesh[:, r * SEG : (r + 1) * SEG]
        sids[GHOST_ROWS + r : GHOST_ROWS + r + 1, :] = send_sub[:, r * SEG : (r + 1) * SEG]

    def take(tables, rows, index):
        low = lax.bitwise_and(index, SEG - 1)
        high = lax.shift_right_logical(index, 7)
        found = [jnp.zeros(index.shape, F32) for _ in range(3)]
        for r in range(rows):
            here = high == r
            for c in range(3):
                source = jnp.broadcast_to(tables[c, r : r + 1, :], index.shape)
                got = jnp.take_along_axis(source, low, axis=1, mode="promise_in_bounds")
                found[c] = jnp.where(here, got, found[c])
        return found

    def halo_copy(src, dst, slot, target):
        return pltpu.make_async_remote_copy(
            src_ref=src,
            dst_ref=dst,
            send_sem=halo_sem.at[slot],
            recv_sem=halo_sem.at[slot + 1],
            device_id=target,
            device_id_type=MESH,
        )

    def velocity_copies(step):
        base = 4 + step * 8
        return (
            halo_copy(v_send_m.at[step], v_recv_m.at[step], base, mesh_next),
            halo_copy(v_send_s.at[step], v_recv_s.at[step], base + 2, sub_next),
        )

    def force_copies(step):
        base = 4 + step * 8 + 4
        return (
            halo_copy(f_send_m.at[step], f_recv_m.at[step], base, mesh_prev),
            halo_copy(f_send_s.at[step], f_recv_s.at[step], base + 2, sub_prev),
        )

    position_copies = (
        halo_copy(p_send_m, p_recv_m, 0, mesh_next),
        halo_copy(p_send_s, p_recv_s, 2, sub_next),
    )

    def stage_velocity(step):
        got = take(vel, own_rows, sids[...])
        for c in range(3):
            v_send_m[step, c] = got[c][:GHOST_ROWS]
            v_send_s[step, c] = got[c][GHOST_ROWS:]

    got = take(pos, own_rows, sids[...])
    for c in range(3):
        p_send_m[c] = got[c][:GHOST_ROWS]
        p_send_s[c] = got[c][GHOST_ROWS:]
    stage_velocity(0)

    pl.semaphore_wait(barrier, peers + 1)
    for copy in position_copies + velocity_copies(0):
        copy.start()

    lax.fori_loop(0, blocks, rows_of_elems, 0)
    for ref in (wtop_b, wlow_b, normals_b):
        ref[...] = jnp.zeros(ref.shape, BF16)

    high_lane = lax.broadcasted_iota(jnp.int32, (16, SEG), 0)
    ghost_lane = lax.bitwise_and(high_lane, 7) + own_rows

    def make_onehot(row, carry):
        lane = lax.broadcasted_iota(jnp.int32, (SEG, SEG), 0)
        for i in range(4):
            index = ids[i, pl.ds(row, 1), :]
            low = lax.bitwise_and(index, SEG - 1)
            high = lax.shift_right_logical(index, 7)
            cols = pl.ds(pl.multiple_of((row * 4 + i) * SEG, SEG), SEG)
            onehot[:, cols] = jnp.where(lane == low, 1.0, 0.0).astype(BF16)
            rowhot[:16, cols] = jnp.where(high_lane == high, 1.0, 0.0).astype(BF16)
            rowhot[16:, cols] = jnp.where(ghost_lane == high, 1.0, 0.0).astype(BF16)
        return carry

    lax.fori_loop(0, blocks, make_onehot, 0)
    for r in range(2 * GHOST_ROWS):
        lane = lax.broadcasted_iota(jnp.int32, (SEG, SEG), 0)
        low = lax.bitwise_and(sids[r : r + 1, :], SEG - 1)
        onehot_back[:, r * SEG : (r + 1) * SEG] = jnp.where(lane == low, 1.0, 0.0).astype(BF16)

    for copy in position_copies:
        copy.wait()
    for c in range(3):
        table[c, :own_rows, :] = pos[c]
        table[c, own_rows : own_rows + GHOST_ROWS, :] = p_recv_m[c]
        table[c, own_rows + GHOST_ROWS :, :] = p_recv_s[c]

    def first_positions(part, carry):
        rows = pl.ds(pl.multiple_of(part * 8, 8), 8)
        for i in range(4):
            got = take(table, own_rows + 2 * GHOST_ROWS, ids[i, rows, :])
            for c in range(3):
                cpos[i, c, rows, :] = got[c]
        return carry

    lax.fori_loop(0, chunks, first_positions, 0)

    def scatter(corners):
        def one_part(part, carry):
            def one_row(r, inner):
                row = part * 8 + r
                values = []
                for i in range(corners):
                    for c in range(3):
                        top = ftop[i, c, pl.ds(row, 1), :]
                        low = flow[i, c, pl.ds(row, 1), :]
                        top8 = jnp.broadcast_to(top, (8, SEG))
                        low8 = jnp.broadcast_to(low, (8, SEG))
                        values.append(
                            (
                                jnp.concatenate([top8, top8], axis=0).astype(BF16),
                                jnp.concatenate([low8, low8], axis=0).astype(BF16),
                                jnp.concatenate([top8, low8], axis=0).astype(BF16),
                            )
                        )
                for i in range(4):
                    cols = pl.ds(pl.multiple_of((row * 4 + i) * SEG, SEG), SEG)
                    at = pl.ds(pl.multiple_of((r * 4 + i) * SEG, SEG), SEG)
                    here = rowhot[:16, cols]
                    away = rowhot[16:, cols]
                    for c in range(3):
                        top, low, both = values[(i if corners > 1 else 0) * 3 + c]
                        spread[c * 32 : c * 32 + 16, at] = here * top
                        spread[c * 32 + 16 : c * 32 + 32, at] = here * low
                        spread[96 + c * 16 : 112 + c * 16, at] = away * both
                return inner

            lax.fori_loop(0, 8, one_row, 0)
            cols = pl.ds(pl.multiple_of(part * 32 * SEG, 32 * SEG), 32 * SEG)
            return carry + dot_nt(spread[...], onehot[:, cols])

        total = lax.fori_loop(0, chunks, one_part, jnp.zeros((144, SEG), F32))
        own = [total[c * 32 : c * 32 + 16] + total[c * 32 + 16 : c * 32 + 32] for c in range(3)]
        ghost = [
            total[96 + c * 16 : 104 + c * 16] + total[104 + c * 16 : 112 + c * 16] for c in range(3)
        ]
        return own + ghost

    def store_halves(i, c, rows, value):
        top = value.astype(BF16).astype(F32)
        ftop[i, c, rows, :] = top
        flow[i, c, rows, :] = value - top

    def one_step(step, step_carry):
        for copy in velocity_copies(step):
            copy.wait()
        for c in range(3):
            vel[c, own_rows : own_rows + GHOST_ROWS, :] = v_recv_m[step, c]
            vel[c, own_rows + GHOST_ROWS :, :] = v_recv_s[step, c]
        advance = jnp.where(step > 0, TIME_STEP, 0.0).astype(F32)

        def shapes(part, carry):
            rows = pl.ds(pl.multiple_of(part * 8, 8), 8)
            a = []
            for i in range(4):
                w = take(vel, own_rows + 2 * GHOST_ROWS, ids[i, rows, :])
                at = []
                for c in range(3):
                    cvel[i, c, rows, :] = w[c]
                    moved = cpos[i, c, rows, :] + advance * w[c]
                    cpos[i, c, rows, :] = moved
                    at.append(moved)
                a.append(at)
            raw = cross(
                [a[2][c] - a[0][c] for c in range(3)], [a[3][c] - a[1][c] for c in range(3)]
            )
            twice = jnp.maximum(jnp.sqrt(dot3(raw, raw)), 1.0)
            area[rows, :] = twice
            for c in range(3):
                n = raw[c] / twice
                centre = 0.25 * (a[0][c] + a[1][c] + a[2][c] + a[3][c])
                nrm[c, rows, :] = n
                geo[rows, c, :] = centre
                geo[rows, 3 + c, :] = n
            return carry

        lax.fori_loop(0, chunks, shapes, 0)

        def block_copy(peer):
            return pltpu.make_async_remote_copy(
                src_ref=send_geo.at[pl.ds(peer * CAP, CAP)],
                dst_ref=recv_geo.at[step, pl.ds(me * CAP, CAP)],
                send_sem=geo_sem.at[0, step],
                recv_sem=geo_sem.at[1, step],
                device_id=(peer, my_sub),
                device_id_type=MESH,
            )

        def send_blocks(peer):
            for c in range(CAP):
                send_geo[peer * CAP + c] = geo[picks[step, peer * CAP + c]]
            block_copy(peer).start()

        each_partner(send_blocks)
        for c in range(CAP):
            recv_geo[step, me * CAP + c] = geo[picks[step, me * CAP + c]]

        def inner_forces(part, carry):
            rows = pl.ds(pl.multiple_of(part * 8, 8), 8)
            a = [[cpos[i, c, rows, :] for c in range(3)] for i in range(4)]
            w = [[cvel[i, c, rows, :] for c in range(3)] for i in range(4)]
            n = [nrm[c, rows, :] for c in range(3)]
            twice = area[rows, :]
            centre = [geo[rows, c, :] for c in range(3)]
            side = [a[1][c] - a[0][c] for c in range(3)]
            length = jnp.maximum(jnp.sqrt(dot3(side, side)), 1.0)
            one = [side[c] / length for c in range(3)]
            two = cross(n, one)
            rel = [[a[i][c] - centre[c] for c in range(3)] for i in range(4)]
            x = [dot3(rel[i], one) for i in range(4)]
            y = [dot3(rel[i], two) for i in range(4)]
            u = [dot3(w[i], one) for i in range(4)]
            v = [dot3(w[i], two) for i in range(4)]
            inverse = 1.0 / twice
            b20, b31 = (y[2] - y[0]) * inverse, (y[1] - y[3]) * inverse
            bx = [b31, b20, -b31, -b20]
            c02, c31 = (x[0] - x[2]) * inverse, (x[3] - x[1]) * inverse
            by = [c31, c02, -c31, -c02]
            exx = b31 * (u[0] - u[2]) + b20 * (u[1] - u[3])
            eyy = c31 * (v[0] - v[2]) + c02 * (v[1] - v[3])
            exy = (
                c31 * (u[0] - u[2]) + c02 * (u[1] - u[3]) + b31 * (v[0] - v[2]) + b20 * (v[1] - v[3])
            )
            s0 = snow[0, rows, :] + TIME_STEP * (PLANE_STIFF * (exx + POISSON * eyy))
            s1 = snow[1, rows, :] + TIME_STEP * (PLANE_STIFF * (POISSON * exx + eyy))
            s2 = snow[2, rows, :] + TIME_STEP * (SHEAR_STIFF * exy)
            snow[0, rows, :] = s0
            snow[1, rows, :] = s1
            snow[2, rows, :] = s2
            half = 0.5 * twice
            hx = x[0] - x[1] + x[2] - x[3]
            hy = y[0] - y[1] + y[2] - y[3]
            signs = (1.0, -1.0, 1.0, -1.0)
            g = [signs[i] - hx * bx[i] - hy * by[i] for i in range(4)]
            r = [
                HOURGLASS * (g[0] * w[0][c] + g[1] * w[1][c] + g[2] * w[2][c] + g[3] * w[3][c])
                for c in range(3)
            ]
            for i in range(4):
                fx = half * (bx[i] * s0 + by[i] * s2)
                fy = half * (by[i] * s1 + bx[i] * s2)
                for c in range(3):
                    store_halves(i, c, rows, -(fx * one[c] + fy * two[c] + g[i] * r[c]))
            return carry

        lax.fori_loop(0, chunks, inner_forces, 0)
        node_force = scatter(4)

        def columns(j, carry):
            for c in range(3):
                row = jnp.broadcast_to(pos[c, pl.ds(j, 1), :], (SEG, SEG))
                pcol[c, j] = jnp.transpose(row)
            for k in range(cands):
                row = pair_mask[step, pl.ds(k, 1), lanes_of(j)].astype(F32) * PENALTY
                mcol[k, j] = jnp.transpose(jnp.broadcast_to(row, (SEG, SEG)))
            return carry

        lax.fori_loop(0, own_rows, columns, 0)

        slot_lane = lax.broadcasted_iota(jnp.int32, (8, slots), 1)
        slot_lane = jnp.where(slot_lane < peers, slot_lane * CAP, (slot_lane - peers) * CAP + 1)

        def name_slots(j, carry):
            for k in range(cands):
                rows = pl.ds(pl.multiple_of((k * own_rows + j) * 8, 8), 8)
                named[rows, :] = jnp.where(slot_lane == buckets[step, k, j], 1.0, 0.0)
            return carry

        lax.fori_loop(0, own_rows, name_slots, 0)
        slot_hot = jnp.transpose(named[...]).astype(BF16)

        everything = pl.ds(0, slots - CAP)
        whole = pltpu.make_async_remote_copy(
            src_ref=send_geo.at[everything],
            dst_ref=recv_geo.at[step, everything],
            send_sem=geo_sem.at[0, step],
            recv_sem=geo_sem.at[1, step],
            device_id=mesh_next,
            device_id_type=MESH,
        )
        whole.wait_recv()

        def contact(j, wtop, wlow, normals_at):
            normals = []
            for k in range(cands):
                block = recv_geo[step, buckets[step, k, j]]
                rows = [jnp.broadcast_to(block[q : q + 1], (16, SEG)) for q in range(6)]
                down = [-rows[3 + c] for c in range(3)]
                normals.append(block[3:6])
                total = jnp.zeros((8, SEG), F32)
                for part in range(SEG // 16):
                    at = slice(part * 16, part * 16 + 16)
                    o = [pcol[c, j, at, :] - rows[c] for c in range(3)]
                    depth = dot3(o, down)
                    reach = depth * depth - dot3(o, o)
                    weight = (
                        jnp.maximum(depth, 0.0) * jnp.exp2(reach * EXP2_SCALE) * mcol[k, j, at, :]
                    )
                    total = total + weight[:8] + weight[8:]
                    top, low = halves(weight)
                    wtop[at, k * SEG : (k + 1) * SEG] = top
                    wlow[at, k * SEG : (k + 1) * SEG] = low
                wsum[pl.ds(pl.multiple_of((k * own_rows + j) * 8, 8), 8), :] = total
            zeros = jnp.zeros((5, cands * SEG), F32)
            flat = jnp.concatenate([jnp.concatenate(normals, axis=1), zeros], axis=0)
            top = flat.astype(BF16).astype(F32)
            normals_at[...] = jnp.concatenate([top, flat - top], axis=0).astype(BF16)

        def push(j, wtop, wlow, normals_at):
            both = normals_at[...]
            force = dot_nt(both, wtop[...])
            rest = dot_nt(both, wlow[...])
            force = force[:8] + force[8:] + rest[:8]
            for c in range(3):
                slave[c, pl.ds(j, 1), :] = force[c : c + 1]

        even = (wtop_a, wlow_a, normals_a)
        odd = (wtop_b, wlow_b, normals_b)

        def contact_pair(half, carry):
            push(jnp.maximum(2 * half - 1, 0), *odd)
            contact(2 * half, *even)
            push(2 * half, *even)
            contact(2 * half + 1, *odd)
            return carry

        lax.fori_loop(0, own_rows // 2, contact_pair, 0)
        push(own_rows - 1, *odd)

        top, low = halves(wsum[...])
        slot_sum = jnp.dot(slot_hot, top, preferred_element_type=F32) + jnp.dot(
            slot_hot, low, preferred_element_type=F32
        )
        for c in range(CAP):
            ret_send[step, :, c, :] = slot_sum[c * peers : (c + 1) * peers]

        def return_copy(peer):
            return pltpu.make_async_remote_copy(
                src_ref=ret_send.at[step, peer],
                dst_ref=ret_recv.at[step, me],
                send_sem=ret_sem.at[0, step],
                recv_sem=ret_sem.at[1, step],
                device_id=(peer, my_sub),
                device_id_type=MESH,
            )

        each_partner(lambda peer: return_copy(peer).start())
        ret_recv[step, me] = ret_send[step, me]
        pick_hot = lax.broadcasted_iota(jnp.int32, (blocks, slots), 0)
        order = lax.broadcasted_iota(jnp.int32, (8, slots), 1)
        order = jnp.where(order < peers, order * CAP, (order - peers) * CAP + 1)
        picked = jnp.broadcast_to(pick_rows[pl.ds(step, 1), :], (8, slots))
        picked = jnp.take_along_axis(picked, order, axis=1, mode="promise_in_bounds")
        pick_hot = jnp.where(pick_hot == picked[:1], 1.0, 0.0).astype(BF16)
        others = pl.ds(0, peers - 1)
        back = pltpu.make_async_remote_copy(
            src_ref=ret_send.at[step, others],
            dst_ref=ret_recv.at[step, others],
            send_sem=ret_sem.at[0, step],
            recv_sem=ret_sem.at[1, step],
            device_id=mesh_next,
            device_id_type=MESH,
        )
        back.wait_recv()
        returned = jnp.concatenate([ret_recv[step, :, c, :] for c in range(CAP)], axis=0)
        top, low = halves(returned)
        press = jnp.dot(pick_hot, top, preferred_element_type=F32) + jnp.dot(
            pick_hot, low, preferred_element_type=F32
        )
        for c in range(3):
            store_halves(0, c, slice(None), -0.25 * nrm[c] * press)
        react = scatter(1)
        force = [node_force[c] + react[c] for c in range(6)]
        for c in range(3):
            f_send_m[step, c] = force[3 + c][:GHOST_ROWS]
            f_send_s[step, c] = force[3 + c][GHOST_ROWS:]
        back_copies = force_copies(step)
        for copy in back_copies:
            copy.start()
        for copy in back_copies:
            copy.wait()
        terms = []
        for c in range(3):
            came = jnp.concatenate([f_recv_m[step, c], f_recv_s[step, c]], axis=0)
            tops, lows = [], []
            for r in range(2 * GHOST_ROWS):
                high = lax.shift_right_logical(sids[r : r + 1, :], 7)
                top, low = halves(jnp.where(high_lane == high, came[r : r + 1], 0.0))
                tops.append(top)
                lows.append(low)
            terms.append(jnp.concatenate(tops, axis=1))
            terms.append(jnp.concatenate(lows, axis=1))
        added = dot_nt(jnp.concatenate(terms, axis=0), onehot_back[...])
        for c in range(3):
            own = force[c]
            own = own + added[c * 32 : c * 32 + own_rows] + added[c * 32 + 16 : c * 32 + 16 + own_rows]
            now = vel[c, :own_rows, :] + TIME_STEP * (own + slave[c]) / mass[...]
            vel[c, :own_rows, :] = now
            pos[c] = pos[c] + TIME_STEP * now
        whole.wait_send()
        back.wait_send()

        @pl.when(step < STEPS - 1)
        def _():
            stage_velocity(step + 1)
            for copy in velocity_copies(step + 1):
                copy.start()

        return step_carry

    lax.fori_loop(0, STEPS, one_step, 0)

    def velocity_lanes(row, carry):
        for c in range(3):
            vel_out[pl.ds(c, 1), lanes_of(row)] = vel[c, pl.ds(row, 1), :]
        return carry

    def stress_lanes(row, carry):
        for c in range(3):
            stress_out[pl.ds(c, 1), lanes_of(row)] = snow[c, pl.ds(row, 1), :]
        return carry

    lax.fori_loop(0, own_rows, velocity_lanes, 0)
    lax.fori_loop(0, blocks, stress_lanes, 0)


def per_device(
    coords, veloc, node_mass, stress, connect, send_mesh, send_sub, send_pick, bucket_list, pair_mask
):
    peers = lax.axis_size("mesh")
    nodes = coords.shape[1]
    elems = stress.shape[1]
    own_rows, blocks = nodes // SEG, elems // SEG
    cands = bucket_list.shape[1]
    slots = send_pick.shape[1]
    pairs = cands * own_rows
    table_rows = own_rows + 2 * GHOST_ROWS
    ghost = (3, GHOST_ROWS, SEG)
    in_vmem = pl.BlockSpec(memory_space=pltpu.VMEM)
    in_smem = pl.BlockSpec(memory_space=pltpu.SMEM)
    v = pltpu.VMEM
    return pl.pallas_call(
        functools.partial(kernel, own_rows, blocks, cands),
        out_shape=(
            jax.ShapeDtypeStruct((3, nodes), F32),
            jax.ShapeDtypeStruct((3, elems), F32),
        ),
        in_specs=[in_vmem] * 7 + [in_smem] * 2 + [in_vmem] * 2,
        out_specs=(in_vmem, in_vmem),
        scratch_shapes=[
            v((4, blocks, SEG), jnp.int32),
            v((2 * GHOST_ROWS, SEG), jnp.int32),
            v((3, own_rows, SEG), F32),
            v((3, table_rows, SEG), F32),
            v((own_rows, SEG), F32),
            v((4, 3, blocks, SEG), F32),
            v((4, 3, blocks, SEG), F32),
            v((3, blocks, SEG), F32),
            v((3, blocks, SEG), F32),
            v((blocks, SEG), F32),
            v((blocks, 6, SEG), F32),
            v((slots, 6, SEG), F32),
            v((STEPS, slots, 6, SEG), F32),
            v((SEG, 4 * elems), BF16),
            v((SEG, 2 * GHOST_ROWS * SEG), BF16),
            v((32, 4 * elems), BF16),
            v((144, 32 * SEG), BF16),
            v((4, 3, blocks, SEG), F32),
            v((4, 3, blocks, SEG), F32),
            v((3, table_rows, SEG), F32),
            v((3, own_rows, SEG, SEG), F32),
            v((cands, own_rows, SEG, SEG), F32),
            v((SEG, cands * SEG), BF16),
            v((SEG, cands * SEG), BF16),
            v((16, cands * SEG), BF16),
            v((SEG, cands * SEG), BF16),
            v((SEG, cands * SEG), BF16),
            v((16, cands * SEG), BF16),
            v((pairs * 8, SEG), F32),
            v((pairs * 8, slots), F32),
            v((3, own_rows, SEG), F32),
            v((STEPS, peers, CAP, SEG), F32),
            v((STEPS, peers, CAP, SEG), F32),
            v(ghost, F32),
            v(ghost, F32),
            v(ghost, F32),
            v(ghost, F32),
            v((STEPS,) + ghost, F32),
            v((STEPS,) + ghost, F32),
            v((STEPS,) + ghost, F32),
            v((STEPS,) + ghost, F32),
            v((STEPS,) + ghost, F32),
            v((STEPS,) + ghost, F32),
            v((STEPS,) + ghost, F32),
            v((STEPS,) + ghost, F32),
            pltpu.SemaphoreType.DMA((4 + STEPS * 8,)),
            pltpu.SemaphoreType.DMA((2, STEPS)),
            pltpu.SemaphoreType.DMA((2, STEPS)),
        ],
        compiler_params=pltpu.CompilerParams(
            collective_id=0, has_side_effects=True, vmem_limit_bytes=56 * 1024 * 1024
        ),
    )(
        coords,
        veloc,
        node_mass.reshape(1, nodes),
        stress,
        connect,
        send_mesh.reshape(1, -1),
        send_sub.reshape(1, -1),
        send_pick,
        bucket_list,
        send_pick,
        pair_mask,
    )


def solution(mesh):
    both = ("mesh", "sub")
    return jax.shard_map(
        per_device,
        mesh=mesh,
        in_specs=(
            P(None, both),
            P(None, both),
            P(both),
            P(None, both),
            P(None, both),
            P(both),
            P(both),
            P(None, both),
            P(None, None, both),
            P(None, None, both),
        ),
        out_specs=(P(None, both), P(None, both)),
        check_vma=False,
    )
```

```python
import functools
import math

import jax
import jax.numpy as jnp
from jax import lax
from jax.experimental import pallas as pl
from jax.experimental.pallas import tpu as pltpu
from jax.sharding import PartitionSpec as P

SEG = 128
STEPS = 4
CAP = 2
TIME_STEP = 0.2
YOUNG = 1.0
POISSON = 0.3
HOURGLASS = 0.01
PENALTY = 0.2
REACH = 4.0
PLANE_STIFF = YOUNG / (1.0 - POISSON * POISSON)
SHEAR_STIFF = YOUNG / (2.0 * (1.0 + POISSON))
EXP2_SCALE = math.log2(math.e) / REACH
ROOT_SCALE = math.sqrt(EXP2_SCALE)
MESH = pl.DeviceIdType.MESH
F32 = jnp.float32
BF16 = jnp.bfloat16
NT = (((1,), (1,)), ((), ()))
GHOST_ROWS = 4


def dot_nt(lhs, rhs):
    return lax.dot_general(lhs, rhs, NT, preferred_element_type=F32)


def halves(value):
    top = value.astype(BF16)
    return top, (value - top.astype(F32)).astype(BF16)


def thirds(value):
    top = value.astype(BF16).astype(F32)
    rest = value - top
    mid = rest.astype(BF16).astype(F32)
    return top, mid, rest - mid


def cross(u, v):
    return (
        u[1] * v[2] - u[2] * v[1],
        u[2] * v[0] - u[0] * v[2],
        u[0] * v[1] - u[1] * v[0],
    )


def dot3(u, v):
    return u[0] * v[0] + u[1] * v[1] + u[2] * v[2]


def kernel(
    own_rows,
    blocks,
    cands,
    coords,
    veloc,
    mass_in,
    stress_in,
    connect,
    send_mesh,
    send_sub,
    picks,
    buckets,
    pick_rows,
    pair_mask,
    vel_out,
    stress_out,
    ids,
    sids,
    pos,
    vel,
    mass,
    cpos,
    cvel,
    snow,
    nrm,
    area,
    geo,
    send_geo,
    recv_geo,
    onehot,
    onehot_back,
    rowhot,
    spread_a,
    spread_b,
    ftop,
    flow,
    table,
    pcol,
    mcol,
    pairs_a,
    pairs_b,
    wtop_a,
    wlow_a,
    normals_a,
    wtop_b,
    wlow_b,
    normals_b,
    wsum,
    named,
    slave,
    ret_send,
    ret_recv,
    first_send_m,
    first_send_s,
    first_recv_m,
    first_recv_s,
    sids_m,
    sids_s,
    same_m,
    same_s,
    values_m,
    values_s,
    part,
    o_send_m,
    o_send_s,
    o_recv_m,
    o_recv_s,
    f_send_m,
    f_send_s,
    f_recv_m,
    f_recv_s,
    x_recv_m,
    x_recv_s,
    halo_sem,
    geo_sem,
    ret_sem,
):
    peers = lax.axis_size("mesh")
    subs = lax.axis_size("sub")
    me = lax.axis_index("mesh")
    my_sub = lax.axis_index("sub")
    mesh_next = (lax.rem(me + 1, peers), my_sub)
    mesh_prev = (lax.rem(me + peers - 1, peers), my_sub)
    sub_next = (me, lax.rem(my_sub + 1, subs))
    sub_prev = (me, lax.rem(my_sub + subs - 1, subs))
    corner_a = (mesh_prev[0], sub_next[1])
    corner_b = (mesh_next[0], sub_prev[1])
    slots = peers * CAP
    chunks = blocks // 8
    pairs = cands * own_rows

    ring_x, ring_z = 4, peers // 8
    my_core, my_z, my_x = me % 2, me // 2 % ring_z, me // (2 * ring_z)

    def spread_out(ring, turn):
        return ring // 2 + (turn + 1) // 2 * (1 - 2 * (turn % 2))

    def each_partner(act):
        def one_z(turn, carry):
            z = lax.rem(my_z + spread_out(ring_z, turn), ring_z)
            for turn_x in range(ring_x):
                x = lax.rem(my_x + spread_out(ring_x, turn_x), ring_x)
                chip = (x * ring_z + z) * 2
                act(chip + 1 - my_core)
                if turn_x < ring_x - 1:
                    act(chip + my_core)
                else:
                    pl.when(turn < ring_z - 1)(lambda chip=chip: act(chip + my_core))
            return carry

        lax.fori_loop(0, ring_z, one_z, 0)

    barrier = pltpu.get_barrier_semaphore()

    def greet(hop, carry):
        pl.semaphore_signal(
            barrier, inc=1, device_id=(lax.rem(me + hop, peers), my_sub), device_id_type=MESH
        )
        return carry

    lax.fori_loop(1, peers, greet, 0)
    for other in (sub_next, sub_prev, corner_a, corner_b):
        pl.semaphore_signal(barrier, inc=1, device_id=other, device_id_type=MESH)

    def lanes_of(row):
        return pl.ds(pl.multiple_of(row * SEG, SEG), SEG)

    def rows_of_nodes(row, carry):
        for c in range(3):
            pos[c, pl.ds(row, 1), :] = coords[pl.ds(c, 1), lanes_of(row)]
            vel[c, pl.ds(row, 1), :] = veloc[pl.ds(c, 1), lanes_of(row)]
        mass[0, pl.ds(row, 1), :] = mass_in[:, lanes_of(row)]
        return carry

    def rows_of_elems(row, carry):
        for c in range(3):
            snow[c, pl.ds(row, 1), :] = stress_in[pl.ds(c, 1), lanes_of(row)]
        for i in range(4):
            ids[i, pl.ds(row, 1), :] = connect[pl.ds(i, 1), lanes_of(row)]
        return carry

    lax.fori_loop(0, own_rows, rows_of_nodes, 0)
    for r in range(GHOST_ROWS):
        sids[r : r + 1, :] = send_mesh[:, r * SEG : (r + 1) * SEG]
        sids[GHOST_ROWS + r : GHOST_ROWS + r + 1, :] = send_sub[:, r * SEG : (r + 1) * SEG]

    def take(tables, rows, index, comps=3):
        low = lax.bitwise_and(index, SEG - 1)
        high = lax.shift_right_logical(index, 7)
        found = [jnp.zeros(index.shape, F32) for _ in range(comps)]
        for r in range(rows):
            here = high == r
            for c in range(comps):
                source = jnp.broadcast_to(tables[c, r : r + 1, :], index.shape)
                got = jnp.take_along_axis(source, low, axis=1, mode="promise_in_bounds")
                found[c] = jnp.where(here, got, found[c])
        return found

    def halo_copy(src, dst, slot, target):
        return pltpu.make_async_remote_copy(
            src_ref=src,
            dst_ref=dst,
            send_sem=halo_sem.at[slot],
            recv_sem=halo_sem.at[slot + 1],
            device_id=target,
            device_id_type=MESH,
        )

    first_copies = (
        halo_copy(first_send_m, first_recv_m, 0, mesh_next),
        halo_copy(first_send_s, first_recv_s, 2, sub_next),
        halo_copy(sids, sids_m, 4, mesh_next),
        halo_copy(sids, sids_s, 6, sub_next),
    )

    def step_copies(step):
        base = 8 + step * 12
        return (
            halo_copy(f_send_m.at[step], x_recv_m.at[step], base, corner_a),
            halo_copy(f_send_s.at[step], x_recv_s.at[step], base + 2, corner_b),
            halo_copy(f_send_m.at[step], f_recv_m.at[step], base + 4, mesh_prev),
            halo_copy(f_send_s.at[step], f_recv_s.at[step], base + 6, sub_prev),
            halo_copy(o_send_m.at[step], o_recv_m.at[step], base + 8, mesh_next),
            halo_copy(o_send_s.at[step], o_recv_s.at[step], base + 10, sub_next),
        )

    firsts = take(pos, own_rows, sids[...]) + take(vel, own_rows, sids[...])
    for q, got in enumerate(firsts + take(mass, own_rows, sids[...], 1)):
        first_send_m[q] = got[:GHOST_ROWS]
        first_send_s[q] = got[GHOST_ROWS:]

    lax.fori_loop(0, blocks, rows_of_elems, 0)
    for ref in (wtop_b, wlow_b, normals_b):
        ref[...] = jnp.zeros(ref.shape, BF16)
    for ref in (values_m, values_s):
        ref[...] = jnp.zeros(ref.shape, F32)

    pl.semaphore_wait(barrier, peers + 3)
    for copy in first_copies:
        copy.start()

    high_lane = lax.broadcasted_iota(jnp.int32, (16, SEG), 0)
    ghost_lane = lax.bitwise_and(high_lane, 7) + own_rows

    def make_onehot(row, carry):
        lane = lax.broadcasted_iota(jnp.int32, (SEG, SEG), 0)
        for i in range(4):
            index = ids[i, pl.ds(row, 1), :]
            low = lax.bitwise_and(index, SEG - 1)
            high = lax.shift_right_logical(index, 7)
            cols = pl.ds(pl.multiple_of((row * 4 + i) * SEG, SEG), SEG)
            onehot[:, cols] = jnp.where(lane == low, 1.0, 0.0).astype(BF16)
            rowhot[:16, cols] = jnp.where(high_lane == high, 1.0, 0.0).astype(BF16)
            rowhot[16:, cols] = jnp.where(ghost_lane == high, 1.0, 0.0).astype(BF16)
        return carry

    lax.fori_loop(0, blocks, make_onehot, 0)
    for r in range(2 * GHOST_ROWS):
        lane = lax.broadcasted_iota(jnp.int32, (SEG, SEG), 0)
        low = lax.bitwise_and(sids[r : r + 1, :], SEG - 1)
        onehot_back[:, r * SEG : (r + 1) * SEG] = jnp.where(lane == low, 1.0, 0.0).astype(BF16)

    for copy in first_copies:
        copy.wait()
    for c in range(3):
        table[c, :own_rows, :] = pos[c]
        for got, at in ((first_recv_m, own_rows), (first_recv_s, own_rows + GHOST_ROWS)):
            table[c, at : at + GHOST_ROWS, :] = got[c]
            vel[c, at : at + GHOST_ROWS, :] = got[3 + c]
    ghost_mass = jnp.concatenate([first_recv_m[6], first_recv_s[6]], axis=0)

    def match(hot, lists, first):
        names = lists[...].astype(F32)
        for q in range(GHOST_ROWS):
            mine = names[first + q : first + q + 1]
            mine = jnp.transpose(jnp.broadcast_to(mine, (SEG, SEG)))
            for r in range(2 * GHOST_ROWS):
                same = jnp.where(mine == names[r : r + 1], 1.0, 0.0)
                hot[q * SEG : (q + 1) * SEG, r * SEG : (r + 1) * SEG] = same.astype(BF16)

    match(same_m, sids_m, 0)
    match(same_s, sids_s, GHOST_ROWS)

    def first_positions(part, carry):
        rows = pl.ds(pl.multiple_of(part * 8, 8), 8)
        for i in range(4):
            got = take(table, own_rows + 2 * GHOST_ROWS, ids[i, rows, :])
            for c in range(3):
                cpos[i, c, rows, :] = got[c]
        return carry

    lax.fori_loop(0, chunks, first_positions, 0)

    def scatter(corners):
        def build(part, spread):
            for r in range(8):
                row = part * 8 + r
                values = []
                for i in range(corners):
                    for c in range(3):
                        top = ftop[i, c, pl.ds(row, 1), :]
                        low = flow[i, c, pl.ds(row, 1), :]
                        top8 = jnp.broadcast_to(top, (8, SEG))
                        low8 = jnp.broadcast_to(low, (8, SEG))
                        values.append(
                            (
                                jnp.concatenate([top8, top8], axis=0).astype(BF16),
                                jnp.concatenate([low8, low8], axis=0).astype(BF16),
                                jnp.concatenate([top8, low8], axis=0).astype(BF16),
                            )
                        )
                for i in range(4):
                    cols = pl.ds(pl.multiple_of((row * 4 + i) * SEG, SEG), SEG)
                    at = slice((r * 4 + i) * SEG, (r * 4 + i + 1) * SEG)
                    here = rowhot[:16, cols]
                    away = rowhot[16:, cols]
                    for c in range(3):
                        top, low, both = values[(i if corners > 1 else 0) * 3 + c]
                        spread[c * 32 : c * 32 + 16, at] = here * top
                        spread[c * 32 + 16 : c * 32 + 32, at] = here * low
                        spread[96 + c * 16 : 112 + c * 16, at] = away * both

        def product(part, spread):
            cols = pl.ds(pl.multiple_of(part * 32 * SEG, 32 * SEG), 32 * SEG)
            return dot_nt(spread[...], onehot[:, cols])

        def two_parts(half, carry):
            build(2 * half + 1, spread_b)
            carry = carry + product(2 * half, spread_a)
            build(jnp.minimum(2 * half + 2, chunks - 1), spread_a)
            return carry + product(2 * half + 1, spread_b)

        build(0, spread_a)
        total = lax.fori_loop(0, chunks // 2, two_parts, jnp.zeros((144, SEG), F32))
        own = [total[c * 32 : c * 32 + 16] + total[c * 32 + 16 : c * 32 + 32] for c in range(3)]
        ghost = [
            total[96 + c * 16 : 104 + c * 16] + total[104 + c * 16 : 112 + c * 16] for c in range(3)
        ]
        return own + ghost

    def store_halves(i, c, rows, value):
        top = value.astype(BF16).astype(F32)
        ftop[i, c, rows, :] = top
        flow[i, c, rows, :] = value - top

    def one_step(step, step_carry):
        advance = jnp.where(step > 0, TIME_STEP, 0.0).astype(F32)

        def shapes(part, carry):
            rows = pl.ds(pl.multiple_of(part * 8, 8), 8)
            a = []
            for i in range(4):
                w = take(vel, own_rows + 2 * GHOST_ROWS, ids[i, rows, :])
                at = []
                for c in range(3):
                    cvel[i, c, rows, :] = w[c]
                    moved = cpos[i, c, rows, :] + advance * w[c]
                    cpos[i, c, rows, :] = moved
                    at.append(moved)
                a.append(at)
            raw = cross(
                [a[2][c] - a[0][c] for c in range(3)], [a[3][c] - a[1][c] for c in range(3)]
            )
            twice = jnp.maximum(jnp.sqrt(dot3(raw, raw)), 1.0)
            area[rows, :] = twice
            for c in range(3):
                n = raw[c] / twice
                centre = 0.25 * (a[0][c] + a[1][c] + a[2][c] + a[3][c])
                nrm[c, rows, :] = n
                geo[rows, c, :] = centre
                geo[rows, 3 + c, :] = n
            return carry

        lax.fori_loop(0, chunks, shapes, 0)

        def block_copy(peer):
            return pltpu.make_async_remote_copy(
                src_ref=send_geo.at[pl.ds(peer * CAP, CAP)],
                dst_ref=recv_geo.at[step, pl.ds(me * CAP, CAP)],
                send_sem=geo_sem.at[0, step],
                recv_sem=geo_sem.at[1, step],
                device_id=(peer, my_sub),
                device_id_type=MESH,
            )

        def send_blocks(peer):
            for c in range(CAP):
                send_geo[peer * CAP + c] = geo[picks[step, peer * CAP + c]]
            block_copy(peer).start()

        each_partner(send_blocks)
        for c in range(CAP):
            recv_geo[step, me * CAP + c] = geo[picks[step, me * CAP + c]]

        def inner_forces(part, carry):
            rows = pl.ds(pl.multiple_of(part * 8, 8), 8)
            a = [[cpos[i, c, rows, :] for c in range(3)] for i in range(4)]
            w = [[cvel[i, c, rows, :] for c in range(3)] for i in range(4)]
            n = [nrm[c, rows, :] for c in range(3)]
            twice = area[rows, :]
            centre = [geo[rows, c, :] for c in range(3)]
            side = [a[1][c] - a[0][c] for c in range(3)]
            length = jnp.maximum(jnp.sqrt(dot3(side, side)), 1.0)
            one = [side[c] / length for c in range(3)]
            two = cross(n, one)
            rel = [[a[i][c] - centre[c] for c in range(3)] for i in range(4)]
            x = [dot3(rel[i], one) for i in range(4)]
            y = [dot3(rel[i], two) for i in range(4)]
            u = [dot3(w[i], one) for i in range(4)]
            v = [dot3(w[i], two) for i in range(4)]
            inverse = 1.0 / twice
            b20, b31 = (y[2] - y[0]) * inverse, (y[1] - y[3]) * inverse
            bx = [b31, b20, -b31, -b20]
            c02, c31 = (x[0] - x[2]) * inverse, (x[3] - x[1]) * inverse
            by = [c31, c02, -c31, -c02]
            exx = b31 * (u[0] - u[2]) + b20 * (u[1] - u[3])
            eyy = c31 * (v[0] - v[2]) + c02 * (v[1] - v[3])
            exy = (
                c31 * (u[0] - u[2]) + c02 * (u[1] - u[3]) + b31 * (v[0] - v[2]) + b20 * (v[1] - v[3])
            )
            s0 = snow[0, rows, :] + TIME_STEP * (PLANE_STIFF * (exx + POISSON * eyy))
            s1 = snow[1, rows, :] + TIME_STEP * (PLANE_STIFF * (POISSON * exx + eyy))
            s2 = snow[2, rows, :] + TIME_STEP * (SHEAR_STIFF * exy)
            snow[0, rows, :] = s0
            snow[1, rows, :] = s1
            snow[2, rows, :] = s2
            half = 0.5 * twice
            hx = x[0] - x[1] + x[2] - x[3]
            hy = y[0] - y[1] + y[2] - y[3]
            signs = (1.0, -1.0, 1.0, -1.0)
            g = [signs[i] - hx * bx[i] - hy * by[i] for i in range(4)]
            r = [
                HOURGLASS * (g[0] * w[0][c] + g[1] * w[1][c] + g[2] * w[2][c] + g[3] * w[3][c])
                for c in range(3)
            ]
            for i in range(4):
                fx = half * (bx[i] * s0 + by[i] * s2)
                fy = half * (by[i] * s1 + bx[i] * s2)
                for c in range(3):
                    store_halves(i, c, rows, -(fx * one[c] + fy * two[c] + g[i] * r[c]))
            return carry

        lax.fori_loop(0, chunks, inner_forces, 0)
        node_force = scatter(4)

        def columns(j, carry):
            p = [pos[c, pl.ds(j, 1), :] for c in range(3)]
            one = jnp.ones((1, SEG), F32)
            top, mid, low = thirds(
                jnp.concatenate(p + [dot3(p, p), one, jnp.zeros((3, SEG), F32)], axis=0)
            )
            pieces = jnp.concatenate([top, top, mid, mid, top, low], axis=0)
            pcol[j] = jnp.transpose(pieces).astype(BF16)
            for k in range(cands):
                row = pair_mask[step, pl.ds(k, 1), lanes_of(j)].astype(F32) * (PENALTY / ROOT_SCALE)
                mcol[k, j] = jnp.transpose(jnp.broadcast_to(row, (SEG, SEG)))
            return carry

        lax.fori_loop(0, own_rows, columns, 0)

        slot_lane = lax.broadcasted_iota(jnp.int32, (8, slots), 1)
        slot_lane = jnp.where(slot_lane < peers, slot_lane * CAP, (slot_lane - peers) * CAP + 1)

        def name_slots(j, carry):
            for k in range(cands):
                rows = pl.ds(pl.multiple_of((k * own_rows + j) * 8, 8), 8)
                named[rows, :] = jnp.where(slot_lane == buckets[step, k, j], 1.0, 0.0)
            return carry

        lax.fori_loop(0, own_rows, name_slots, 0)
        slot_hot = jnp.transpose(named[...]).astype(BF16)

        everything = pl.ds(0, slots - CAP)
        whole = pltpu.make_async_remote_copy(
            src_ref=send_geo.at[everything],
            dst_ref=recv_geo.at[step, everything],
            send_sem=geo_sem.at[0, step],
            recv_sem=geo_sem.at[1, step],
            device_id=mesh_next,
            device_id_type=MESH,
        )
        whole.wait_recv()

        def quadratics(j, both):
            for k in range(cands):
                block = recv_geo[step, buckets[step, k, j]]
                centre, normal = block[:3], block[3:6]
                along = jnp.sum(centre * normal, axis=0, keepdims=True)
                square = jnp.sum(centre * centre, axis=0, keepdims=True)
                nothing = jnp.zeros((1, SEG), F32)
                blank = jnp.zeros((3, SEG), F32)
                depth = jnp.concatenate([-normal, nothing, along, blank], axis=0) * ROOT_SCALE
                far = jnp.concatenate([-2.0 * centre, nothing + 1.0, square, blank], axis=0)
                top, mid, low = thirds(jnp.concatenate([depth, far * EXP2_SCALE], axis=1))
                pieces = jnp.concatenate([top, mid, top, mid, low, top], axis=0).astype(BF16)
                at = slice(k * 2 * SEG, (k + 1) * 2 * SEG)
                both[:, at] = jnp.dot(pcol[j], pieces, preferred_element_type=F32)

        def contact(j, both, wtop, wlow, normals_at):
            normals = []
            for k in range(cands):
                normals.append(recv_geo[step, buckets[step, k, j]][3:6])
                total = jnp.zeros((8, SEG), F32)
                for part in range(SEG // 16):
                    at = slice(part * 16, part * 16 + 16)
                    depth = both[at, k * 2 * SEG : (k * 2 + 1) * SEG]
                    far = both[at, (k * 2 + 1) * SEG : (k * 2 + 2) * SEG]
                    weight = (
                        jnp.maximum(depth, 0.0) * jnp.exp2(depth * depth - far) * mcol[k, j, at, :]
                    )
                    total = total + weight[:8] + weight[8:]
                    top, low = halves(weight)
                    wtop[at, k * SEG : (k + 1) * SEG] = top
                    wlow[at, k * SEG : (k + 1) * SEG] = low
                wsum[pl.ds(pl.multiple_of((k * own_rows + j) * 8, 8), 8), :] = total
            zeros = jnp.zeros((5, cands * SEG), F32)
            flat = jnp.concatenate([jnp.concatenate(normals, axis=1), zeros], axis=0)
            top = flat.astype(BF16).astype(F32)
            normals_at[...] = jnp.concatenate([top, flat - top], axis=0).astype(BF16)

        def push(j, wtop, wlow, normals_at):
            both = normals_at[...]
            force = dot_nt(both, wtop[...])
            rest = dot_nt(both, wlow[...])
            force = force[:8] + force[8:] + rest[:8]
            for c in range(3):
                slave[c, pl.ds(j, 1), :] = force[c : c + 1]

        even = (wtop_a, wlow_a, normals_a)
        odd = (wtop_b, wlow_b, normals_b)

        def contact_pair(half, carry):
            quadratics(2 * half + 1, pairs_b)
            push(jnp.maximum(2 * half - 1, 0), *odd)
            contact(2 * half, pairs_a, *even)
            quadratics(jnp.minimum(2 * half + 2, own_rows - 1), pairs_a)
            push(2 * half, *even)
            contact(2 * half + 1, pairs_b, *odd)
            return carry

        quadratics(0, pairs_a)

        lax.fori_loop(0, own_rows // 2, contact_pair, 0)
        push(own_rows - 1, *odd)

        top, low = halves(wsum[...])
        slot_sum = jnp.dot(slot_hot, top, preferred_element_type=F32) + jnp.dot(
            slot_hot, low, preferred_element_type=F32
        )
        for c in range(CAP):
            ret_send[step, :, c, :] = slot_sum[c * peers : (c + 1) * peers]

        def return_copy(peer):
            return pltpu.make_async_remote_copy(
                src_ref=ret_send.at[step, peer],
                dst_ref=ret_recv.at[step, me],
                send_sem=ret_sem.at[0, step],
                recv_sem=ret_sem.at[1, step],
                device_id=(peer, my_sub),
                device_id_type=MESH,
            )

        each_partner(lambda peer: return_copy(peer).start())
        ret_recv[step, me] = ret_send[step, me]
        pick_hot = lax.broadcasted_iota(jnp.int32, (blocks, slots), 0)
        order = lax.broadcasted_iota(jnp.int32, (8, slots), 1)
        order = jnp.where(order < peers, order * CAP, (order - peers) * CAP + 1)
        picked = jnp.broadcast_to(pick_rows[pl.ds(step, 1), :], (8, slots))
        picked = jnp.take_along_axis(picked, order, axis=1, mode="promise_in_bounds")
        pick_hot = jnp.where(pick_hot == picked[:1], 1.0, 0.0).astype(BF16)
        others = pl.ds(0, peers - 1)
        back = pltpu.make_async_remote_copy(
            src_ref=ret_send.at[step, others],
            dst_ref=ret_recv.at[step, others],
            send_sem=ret_sem.at[0, step],
            recv_sem=ret_sem.at[1, step],
            device_id=mesh_next,
            device_id_type=MESH,
        )
        back.wait_recv()
        returned = jnp.concatenate([ret_recv[step, :, c, :] for c in range(CAP)], axis=0)
        top, low = halves(returned)
        press = jnp.dot(pick_hot, top, preferred_element_type=F32) + jnp.dot(
            pick_hot, low, preferred_element_type=F32
        )
        for c in range(3):
            store_halves(0, c, slice(None), -0.25 * nrm[c] * press)
        react = scatter(1)
        force = [node_force[c] + react[c] for c in range(6)]
        for c in range(3):
            f_send_m[step, c] = force[3 + c][:GHOST_ROWS]
            f_send_s[step, c] = force[3 + c][GHOST_ROWS:]
            part[c] = force[c] + slave[c]
        shared = take(part, own_rows, sids[...])
        for c in range(3):
            o_send_m[step, c] = shared[c][:GHOST_ROWS]
            o_send_s[step, c] = shared[c][GHOST_ROWS:]
        back_copies = step_copies(step)
        for copy in back_copies:
            copy.start()
        for copy in back_copies:
            copy.wait()

        def ghost_sum(values, hot, from_mesh, from_sub):
            for c in range(3):
                for r in range(GHOST_ROWS):
                    values[c : c + 1, r * SEG : (r + 1) * SEG] = from_mesh[step, c, r : r + 1]
                    at = (GHOST_ROWS + r) * SEG
                    values[c : c + 1, at : at + SEG] = from_sub[step, c, r : r + 1]
            top = values[...].astype(BF16).astype(F32)
            both = jnp.concatenate([top, values[...] - top], axis=0).astype(BF16)
            total = dot_nt(both, hot[...])
            return total[:8] + total[8:]

        sum_m = ghost_sum(values_m, same_m, f_send_m, x_recv_s)
        sum_s = ghost_sum(values_s, same_s, x_recv_m, f_send_s)
        for c in range(3):
            rows = [sum_m[c : c + 1, r * SEG : (r + 1) * SEG] for r in range(GHOST_ROWS)]
            rows += [sum_s[c : c + 1, r * SEG : (r + 1) * SEG] for r in range(GHOST_ROWS)]
            owned = jnp.concatenate([o_recv_m[step, c], o_recv_s[step, c]], axis=0)
            total = owned + jnp.concatenate(rows, axis=0)
            vel[c, own_rows:, :] = vel[c, own_rows:, :] + TIME_STEP * total / ghost_mass
        terms = []
        for c in range(3):
            came = jnp.concatenate([f_recv_m[step, c], f_recv_s[step, c]], axis=0)
            tops, lows = [], []
            for r in range(2 * GHOST_ROWS):
                high = lax.shift_right_logical(sids[r : r + 1, :], 7)
                top, low = halves(jnp.where(high_lane == high, came[r : r + 1], 0.0))
                tops.append(top)
                lows.append(low)
            terms.append(jnp.concatenate(tops, axis=1))
            terms.append(jnp.concatenate(lows, axis=1))
        added = dot_nt(jnp.concatenate(terms, axis=0), onehot_back[...])
        for c in range(3):
            own = part[c] + added[c * 32 : c * 32 + own_rows] + added[c * 32 + 16 : c * 32 + 16 + own_rows]
            now = vel[c, :own_rows, :] + TIME_STEP * own / mass[0]
            vel[c, :own_rows, :] = now
            pos[c] = pos[c] + TIME_STEP * now
        whole.wait_send()
        back.wait_send()

        return step_carry

    lax.fori_loop(0, STEPS, one_step, 0)

    def velocity_lanes(row, carry):
        for c in range(3):
            vel_out[pl.ds(c, 1), lanes_of(row)] = vel[c, pl.ds(row, 1), :]
        return carry

    def stress_lanes(row, carry):
        for c in range(3):
            stress_out[pl.ds(c, 1), lanes_of(row)] = snow[c, pl.ds(row, 1), :]
        return carry

    lax.fori_loop(0, own_rows, velocity_lanes, 0)
    lax.fori_loop(0, blocks, stress_lanes, 0)


def per_device(
    coords, veloc, node_mass, stress, connect, send_mesh, send_sub, send_pick, bucket_list, pair_mask
):
    peers = lax.axis_size("mesh")
    nodes = coords.shape[1]
    elems = stress.shape[1]
    own_rows, blocks = nodes // SEG, elems // SEG
    cands = bucket_list.shape[1]
    slots = send_pick.shape[1]
    pairs = cands * own_rows
    table_rows = own_rows + 2 * GHOST_ROWS
    in_vmem = pl.BlockSpec(memory_space=pltpu.VMEM)
    in_smem = pl.BlockSpec(memory_space=pltpu.SMEM)
    v = pltpu.VMEM
    return pl.pallas_call(
        functools.partial(kernel, own_rows, blocks, cands),
        out_shape=(
            jax.ShapeDtypeStruct((3, nodes), F32),
            jax.ShapeDtypeStruct((3, elems), F32),
        ),
        in_specs=[in_vmem] * 7 + [in_smem] * 2 + [in_vmem] * 2,
        out_specs=(in_vmem, in_vmem),
        scratch_shapes=[
            v((4, blocks, SEG), jnp.int32),
            v((2 * GHOST_ROWS, SEG), jnp.int32),
            v((3, own_rows, SEG), F32),
            v((3, table_rows, SEG), F32),
            v((1, own_rows, SEG), F32),
            v((4, 3, blocks, SEG), F32),
            v((4, 3, blocks, SEG), F32),
            v((3, blocks, SEG), F32),
            v((3, blocks, SEG), F32),
            v((blocks, SEG), F32),
            v((blocks, 6, SEG), F32),
            v((slots, 6, SEG), F32),
            v((STEPS, slots, 6, SEG), F32),
            v((SEG, 4 * elems), BF16),
            v((SEG, 2 * GHOST_ROWS * SEG), BF16),
            v((32, 4 * elems), BF16),
            *[v((144, 32 * SEG), BF16)] * 2,
            v((4, 3, blocks, SEG), F32),
            v((4, 3, blocks, SEG), F32),
            v((3, table_rows, SEG), F32),
            v((own_rows, SEG, 48), BF16),
            v((cands, own_rows, SEG, SEG), F32),
            v((SEG, cands * 2 * SEG), F32),
            v((SEG, cands * 2 * SEG), F32),
            v((SEG, cands * SEG), BF16),
            v((SEG, cands * SEG), BF16),
            v((16, cands * SEG), BF16),
            v((SEG, cands * SEG), BF16),
            v((SEG, cands * SEG), BF16),
            v((16, cands * SEG), BF16),
            v((pairs * 8, SEG), F32),
            v((pairs * 8, slots), F32),
            v((3, own_rows, SEG), F32),
            v((STEPS, peers, CAP, SEG), F32),
            v((STEPS, peers, CAP, SEG), F32),
            *[v((7, GHOST_ROWS, SEG), F32)] * 4,
            *[v((2 * GHOST_ROWS, SEG), jnp.int32)] * 2,
            *[v((GHOST_ROWS * SEG, 2 * GHOST_ROWS * SEG), BF16)] * 2,
            *[v((8, 2 * GHOST_ROWS * SEG), F32)] * 2,
            v((3, own_rows, SEG), F32),
            *[v((STEPS, 3, GHOST_ROWS, SEG), F32)] * 10,
            pltpu.SemaphoreType.DMA((8 + STEPS * 12,)),
            pltpu.SemaphoreType.DMA((2, STEPS)),
            pltpu.SemaphoreType.DMA((2, STEPS)),
        ],
        compiler_params=pltpu.CompilerParams(
            collective_id=0, has_side_effects=True, vmem_limit_bytes=56 * 1024 * 1024
        ),
    )(
        coords,
        veloc,
        node_mass.reshape(1, nodes),
        stress,
        connect,
        send_mesh.reshape(1, -1),
        send_sub.reshape(1, -1),
        send_pick,
        bucket_list,
        send_pick,
        pair_mask,
    )


def solution(mesh):
    both = ("mesh", "sub")
    return jax.shard_map(
        per_device,
        mesh=mesh,
        in_specs=(
            P(None, both),
            P(None, both),
            P(both),
            P(None, both),
            P(None, both),
            P(both),
            P(both),
            P(None, both),
            P(None, None, both),
            P(None, None, both),
        ),
        out_specs=(P(None, both), P(None, both)),
        check_vma=False,
    )
```

```python
import functools
import math

import jax
import jax.numpy as jnp
from jax import lax
from jax.experimental import pallas as pl
from jax.experimental.pallas import tpu as pltpu
from jax.sharding import PartitionSpec as P

SEG = 128
STEPS = 4
CAP = 2
TIME_STEP = 0.2
YOUNG = 1.0
POISSON = 0.3
HOURGLASS = 0.01
PENALTY = 0.2
REACH = 4.0
PLANE_STIFF = YOUNG / (1.0 - POISSON * POISSON)
SHEAR_STIFF = YOUNG / (2.0 * (1.0 + POISSON))
EXP2_SCALE = math.log2(math.e) / REACH
ROOT_SCALE = math.sqrt(EXP2_SCALE)
MESH = pl.DeviceIdType.MESH
F32 = jnp.float32
BF16 = jnp.bfloat16
NT = (((1,), (1,)), ((), ()))
GHOST_ROWS = 4


def dot_nt(lhs, rhs):
    return lax.dot_general(lhs, rhs, NT, preferred_element_type=F32)


def halves(value):
    top = value.astype(BF16)
    return top, (value - top.astype(F32)).astype(BF16)


def thirds(value):
    top = value.astype(BF16).astype(F32)
    rest = value - top
    mid = rest.astype(BF16).astype(F32)
    return top, mid, rest - mid


def cross(u, v):
    return (
        u[1] * v[2] - u[2] * v[1],
        u[2] * v[0] - u[0] * v[2],
        u[0] * v[1] - u[1] * v[0],
    )


def dot3(u, v):
    return u[0] * v[0] + u[1] * v[1] + u[2] * v[2]


def kernel(
    own_rows,
    blocks,
    cands,
    coords,
    veloc,
    mass_in,
    stress_in,
    connect,
    send_mesh,
    send_sub,
    picks,
    buckets,
    pick_rows,
    pair_mask,
    vel_out,
    stress_out,
    ids,
    sids,
    pos,
    vel,
    mass,
    cpos,
    cvel,
    snow,
    nrm,
    area,
    geo,
    send_geo,
    recv_geo,
    onehot,
    onehot_back,
    rowhot,
    spread_a,
    spread_b,
    ftop,
    flow,
    table,
    pcol,
    mcol,
    pairs_a,
    pairs_b,
    wtop_a,
    wlow_a,
    normals_a,
    wtop_b,
    wlow_b,
    normals_b,
    wsum,
    named,
    slave,
    ret_send,
    ret_recv,
    first_send_m,
    first_send_s,
    first_recv_m,
    first_recv_s,
    sids_m,
    sids_s,
    same_m,
    same_s,
    values_m,
    values_s,
    part,
    o_send_m,
    o_send_s,
    o_recv_m,
    o_recv_s,
    f_send_m,
    f_send_s,
    f_recv_m,
    f_recv_s,
    x_recv_m,
    x_recv_s,
    halo_sem,
    geo_sem,
    ret_sem,
):
    peers = lax.axis_size("mesh")
    subs = lax.axis_size("sub")
    me = lax.axis_index("mesh")
    my_sub = lax.axis_index("sub")
    mesh_next = (lax.rem(me + 1, peers), my_sub)
    mesh_prev = (lax.rem(me + peers - 1, peers), my_sub)
    sub_next = (me, lax.rem(my_sub + 1, subs))
    sub_prev = (me, lax.rem(my_sub + subs - 1, subs))
    corner_a = (mesh_prev[0], sub_next[1])
    corner_b = (mesh_next[0], sub_prev[1])
    slots = peers * CAP
    chunks = blocks // 8
    pairs = cands * own_rows

    ring_x, ring_z = 4, peers // 8
    my_core, my_z, my_x = me % 2, me // 2 % ring_z, me // (2 * ring_z)

    def spread_out(ring, turn):
        return ring // 2 + (turn + 1) // 2 * (1 - 2 * (turn % 2))

    def each_partner(act):
        def one_x(turn, carry):
            x = lax.rem(my_x + spread_out(ring_x, turn), ring_x)
            for turn_z in range(ring_z):
                z = lax.rem(my_z + spread_out(ring_z, turn_z), ring_z)
                chip = (x * ring_z + z) * 2
                act(chip + 1 - my_core)
                if turn_z < ring_z - 1:
                    act(chip + my_core)
                else:
                    pl.when(turn < ring_x - 1)(lambda chip=chip: act(chip + my_core))
            return carry

        lax.fori_loop(0, ring_x, one_x, 0)

    barrier = pltpu.get_barrier_semaphore()

    def greet(hop, carry):
        pl.semaphore_signal(
            barrier, inc=1, device_id=(lax.rem(me + hop, peers), my_sub), device_id_type=MESH
        )
        return carry

    lax.fori_loop(1, peers, greet, 0)
    for other in (sub_next, sub_prev, corner_a, corner_b):
        pl.semaphore_signal(barrier, inc=1, device_id=other, device_id_type=MESH)

    def lanes_of(row):
        return pl.ds(pl.multiple_of(row * SEG, SEG), SEG)

    def rows_of_nodes(row, carry):
        for c in range(3):
            pos[c, pl.ds(row, 1), :] = coords[pl.ds(c, 1), lanes_of(row)]
            vel[c, pl.ds(row, 1), :] = veloc[pl.ds(c, 1), lanes_of(row)]
        mass[0, pl.ds(row, 1), :] = mass_in[:, lanes_of(row)]
        return carry

    def rows_of_elems(row, carry):
        for c in range(3):
            snow[c, pl.ds(row, 1), :] = stress_in[pl.ds(c, 1), lanes_of(row)]
        for i in range(4):
            ids[i, pl.ds(row, 1), :] = connect[pl.ds(i, 1), lanes_of(row)]
        return carry

    lax.fori_loop(0, own_rows, rows_of_nodes, 0)
    for r in range(GHOST_ROWS):
        sids[r : r + 1, :] = send_mesh[:, r * SEG : (r + 1) * SEG]
        sids[GHOST_ROWS + r : GHOST_ROWS + r + 1, :] = send_sub[:, r * SEG : (r + 1) * SEG]

    def take(tables, rows, index, comps=3):
        low = lax.bitwise_and(index, SEG - 1)
        high = lax.shift_right_logical(index, 7)
        found = [jnp.zeros(index.shape, F32) for _ in range(comps)]
        for r in range(rows):
            here = high == r
            for c in range(comps):
                source = jnp.broadcast_to(tables[c, r : r + 1, :], index.shape)
                got = jnp.take_along_axis(source, low, axis=1, mode="promise_in_bounds")
                found[c] = jnp.where(here, got, found[c])
        return found

    def halo_copy(src, dst, slot, target):
        return pltpu.make_async_remote_copy(
            src_ref=src,
            dst_ref=dst,
            send_sem=halo_sem.at[slot],
            recv_sem=halo_sem.at[slot + 1],
            device_id=target,
            device_id_type=MESH,
        )

    first_copies = (
        halo_copy(first_send_m, first_recv_m, 0, mesh_next),
        halo_copy(first_send_s, first_recv_s, 2, sub_next),
        halo_copy(sids, sids_m, 4, mesh_next),
        halo_copy(sids, sids_s, 6, sub_next),
    )

    def step_copies(step):
        base = 8 + step * 12
        return (
            halo_copy(f_send_m.at[step], x_recv_m.at[step], base, corner_a),
            halo_copy(f_send_s.at[step], x_recv_s.at[step], base + 2, corner_b),
            halo_copy(f_send_m.at[step], f_recv_m.at[step], base + 4, mesh_prev),
            halo_copy(f_send_s.at[step], f_recv_s.at[step], base + 6, sub_prev),
            halo_copy(o_send_m.at[step], o_recv_m.at[step], base + 8, mesh_next),
            halo_copy(o_send_s.at[step], o_recv_s.at[step], base + 10, sub_next),
        )

    firsts = take(pos, own_rows, sids[...]) + take(vel, own_rows, sids[...])
    for q, got in enumerate(firsts + take(mass, own_rows, sids[...], 1)):
        first_send_m[q] = got[:GHOST_ROWS]
        first_send_s[q] = got[GHOST_ROWS:]

    lax.fori_loop(0, blocks, rows_of_elems, 0)
    for ref in (wtop_b, wlow_b, normals_b):
        ref[...] = jnp.zeros(ref.shape, BF16)
    for ref in (values_m, values_s):
        ref[...] = jnp.zeros(ref.shape, F32)

    pl.semaphore_wait(barrier, peers + 3)
    for copy in first_copies:
        copy.start()

    high_lane = lax.broadcasted_iota(jnp.int32, (16, SEG), 0)
    ghost_lane = lax.bitwise_and(high_lane, 7) + own_rows

    def make_onehot(row, carry):
        lane = lax.broadcasted_iota(jnp.int32, (SEG, SEG), 0)
        for i in range(4):
            index = ids[i, pl.ds(row, 1), :]
            low = lax.bitwise_and(index, SEG - 1)
            high = lax.shift_right_logical(index, 7)
            cols = pl.ds(pl.multiple_of((row * 4 + i) * SEG, SEG), SEG)
            onehot[:, cols] = jnp.where(lane == low, 1.0, 0.0).astype(BF16)
            rowhot[:16, cols] = jnp.where(high_lane == high, 1.0, 0.0).astype(BF16)
            rowhot[16:, cols] = jnp.where(ghost_lane == high, 1.0, 0.0).astype(BF16)
        return carry

    lax.fori_loop(0, blocks, make_onehot, 0)
    for r in range(2 * GHOST_ROWS):
        lane = lax.broadcasted_iota(jnp.int32, (SEG, SEG), 0)
        low = lax.bitwise_and(sids[r : r + 1, :], SEG - 1)
        onehot_back[:, r * SEG : (r + 1) * SEG] = jnp.where(lane == low, 1.0, 0.0).astype(BF16)

    for copy in first_copies:
        copy.wait()
    for c in range(3):
        table[c, :own_rows, :] = pos[c]
        for got, at in ((first_recv_m, own_rows), (first_recv_s, own_rows + GHOST_ROWS)):
            table[c, at : at + GHOST_ROWS, :] = got[c]
            vel[c, at : at + GHOST_ROWS, :] = got[3 + c]
    ghost_mass = jnp.concatenate([first_recv_m[6], first_recv_s[6]], axis=0)

    def match(hot, lists, first):
        names = lists[...].astype(F32)
        for q in range(GHOST_ROWS):
            mine = names[first + q : first + q + 1]
            mine = jnp.transpose(jnp.broadcast_to(mine, (SEG, SEG)))
            for r in range(2 * GHOST_ROWS):
                same = jnp.where(mine == names[r : r + 1], 1.0, 0.0)
                hot[q * SEG : (q + 1) * SEG, r * SEG : (r + 1) * SEG] = same.astype(BF16)

    match(same_m, sids_m, 0)
    match(same_s, sids_s, GHOST_ROWS)

    def first_positions(part, carry):
        rows = pl.ds(pl.multiple_of(part * 8, 8), 8)
        for i in range(4):
            got = take(table, own_rows + 2 * GHOST_ROWS, ids[i, rows, :])
            for c in range(3):
                cpos[i, c, rows, :] = got[c]
        return carry

    lax.fori_loop(0, chunks, first_positions, 0)

    def scatter(corners):
        def build(part, spread):
            for r in range(8):
                row = part * 8 + r
                values = []
                for i in range(corners):
                    for c in range(3):
                        top = ftop[i, c, pl.ds(row, 1), :]
                        low = flow[i, c, pl.ds(row, 1), :]
                        top8 = jnp.broadcast_to(top, (8, SEG))
                        low8 = jnp.broadcast_to(low, (8, SEG))
                        values.append(
                            (
                                jnp.concatenate([top8, top8], axis=0).astype(BF16),
                                jnp.concatenate([low8, low8], axis=0).astype(BF16),
                                jnp.concatenate([top8, low8], axis=0).astype(BF16),
                            )
                        )
                for i in range(4):
                    cols = pl.ds(pl.multiple_of((row * 4 + i) * SEG, SEG), SEG)
                    at = slice((r * 4 + i) * SEG, (r * 4 + i + 1) * SEG)
                    here = rowhot[:16, cols]
                    away = rowhot[16:, cols]
                    for c in range(3):
                        top, low, both = values[(i if corners > 1 else 0) * 3 + c]
                        spread[c * 32 : c * 32 + 16, at] = here * top
                        spread[c * 32 + 16 : c * 32 + 32, at] = here * low
                        spread[96 + c * 16 : 112 + c * 16, at] = away * both

        def product(part, spread):
            cols = pl.ds(pl.multiple_of(part * 32 * SEG, 32 * SEG), 32 * SEG)
            return dot_nt(spread[...], onehot[:, cols])

        def two_parts(half, carry):
            build(2 * half + 1, spread_b)
            carry = carry + product(2 * half, spread_a)
            build(jnp.minimum(2 * half + 2, chunks - 1), spread_a)
            return carry + product(2 * half + 1, spread_b)

        build(0, spread_a)
        total = lax.fori_loop(0, chunks // 2, two_parts, jnp.zeros((144, SEG), F32))
        own = [total[c * 32 : c * 32 + 16] + total[c * 32 + 16 : c * 32 + 32] for c in range(3)]
        ghost = [
            total[96 + c * 16 : 104 + c * 16] + total[104 + c * 16 : 112 + c * 16] for c in range(3)
        ]
        return own + ghost

    def store_halves(i, c, rows, value):
        top = value.astype(BF16).astype(F32)
        ftop[i, c, rows, :] = top
        flow[i, c, rows, :] = value - top

    def one_step(step, step_carry):
        advance = jnp.where(step > 0, TIME_STEP, 0.0).astype(F32)

        def shapes(part, carry):
            rows = pl.ds(pl.multiple_of(part * 8, 8), 8)
            a = []
            for i in range(4):
                w = take(vel, own_rows + 2 * GHOST_ROWS, ids[i, rows, :])
                at = []
                for c in range(3):
                    cvel[i, c, rows, :] = w[c]
                    moved = cpos[i, c, rows, :] + advance * w[c]
                    cpos[i, c, rows, :] = moved
                    at.append(moved)
                a.append(at)
            raw = cross(
                [a[2][c] - a[0][c] for c in range(3)], [a[3][c] - a[1][c] for c in range(3)]
            )
            twice = jnp.maximum(jnp.sqrt(dot3(raw, raw)), 1.0)
            area[rows, :] = twice
            for c in range(3):
                n = raw[c] / twice
                centre = 0.25 * (a[0][c] + a[1][c] + a[2][c] + a[3][c])
                nrm[c, rows, :] = n
                geo[rows, c, :] = centre
                geo[rows, 3 + c, :] = n
            return carry

        lax.fori_loop(0, chunks, shapes, 0)

        def block_copy(peer):
            return pltpu.make_async_remote_copy(
                src_ref=send_geo.at[pl.ds(peer * CAP, CAP)],
                dst_ref=recv_geo.at[step, pl.ds(me * CAP, CAP)],
                send_sem=geo_sem.at[0, step],
                recv_sem=geo_sem.at[1, step],
                device_id=(peer, my_sub),
                device_id_type=MESH,
            )

        def send_blocks(peer):
            for c in range(CAP):
                send_geo[peer * CAP + c] = geo[picks[step, peer * CAP + c]]
            block_copy(peer).start()

        each_partner(send_blocks)
        for c in range(CAP):
            recv_geo[step, me * CAP + c] = geo[picks[step, me * CAP + c]]

        def inner_forces(part, carry):
            rows = pl.ds(pl.multiple_of(part * 8, 8), 8)
            a = [[cpos[i, c, rows, :] for c in range(3)] for i in range(4)]
            w = [[cvel[i, c, rows, :] for c in range(3)] for i in range(4)]
            n = [nrm[c, rows, :] for c in range(3)]
            twice = area[rows, :]
            centre = [geo[rows, c, :] for c in range(3)]
            side = [a[1][c] - a[0][c] for c in range(3)]
            length = jnp.maximum(jnp.sqrt(dot3(side, side)), 1.0)
            one = [side[c] / length for c in range(3)]
            two = cross(n, one)
            rel = [[a[i][c] - centre[c] for c in range(3)] for i in range(4)]
            x = [dot3(rel[i], one) for i in range(4)]
            y = [dot3(rel[i], two) for i in range(4)]
            u = [dot3(w[i], one) for i in range(4)]
            v = [dot3(w[i], two) for i in range(4)]
            inverse = 1.0 / twice
            b20, b31 = (y[2] - y[0]) * inverse, (y[1] - y[3]) * inverse
            bx = [b31, b20, -b31, -b20]
            c02, c31 = (x[0] - x[2]) * inverse, (x[3] - x[1]) * inverse
            by = [c31, c02, -c31, -c02]
            exx = b31 * (u[0] - u[2]) + b20 * (u[1] - u[3])
            eyy = c31 * (v[0] - v[2]) + c02 * (v[1] - v[3])
            exy = (
                c31 * (u[0] - u[2]) + c02 * (u[1] - u[3]) + b31 * (v[0] - v[2]) + b20 * (v[1] - v[3])
            )
            s0 = snow[0, rows, :] + TIME_STEP * (PLANE_STIFF * (exx + POISSON * eyy))
            s1 = snow[1, rows, :] + TIME_STEP * (PLANE_STIFF * (POISSON * exx + eyy))
            s2 = snow[2, rows, :] + TIME_STEP * (SHEAR_STIFF * exy)
            snow[0, rows, :] = s0
            snow[1, rows, :] = s1
            snow[2, rows, :] = s2
            half = 0.5 * twice
            hx = x[0] - x[1] + x[2] - x[3]
            hy = y[0] - y[1] + y[2] - y[3]
            signs = (1.0, -1.0, 1.0, -1.0)
            g = [signs[i] - hx * bx[i] - hy * by[i] for i in range(4)]
            r = [
                HOURGLASS * (g[0] * w[0][c] + g[1] * w[1][c] + g[2] * w[2][c] + g[3] * w[3][c])
                for c in range(3)
            ]
            for i in range(4):
                fx = half * (bx[i] * s0 + by[i] * s2)
                fy = half * (by[i] * s1 + bx[i] * s2)
                for c in range(3):
                    store_halves(i, c, rows, -(fx * one[c] + fy * two[c] + g[i] * r[c]))
            return carry

        lax.fori_loop(0, chunks, inner_forces, 0)
        node_force = scatter(4)

        def columns(j, carry):
            p = [pos[c, pl.ds(j, 1), :] for c in range(3)]
            one = jnp.ones((1, SEG), F32)
            top, mid, low = thirds(
                jnp.concatenate(p + [dot3(p, p), one, jnp.zeros((3, SEG), F32)], axis=0)
            )
            pieces = jnp.concatenate([top, top, mid, mid, top, low], axis=0)
            pcol[j] = jnp.transpose(pieces).astype(BF16)
            for k in range(cands):
                row = pair_mask[step, pl.ds(k, 1), lanes_of(j)].astype(F32) * (PENALTY / ROOT_SCALE)
                mcol[k, j] = jnp.transpose(jnp.broadcast_to(row, (SEG, SEG)))
            return carry

        lax.fori_loop(0, own_rows, columns, 0)

        slot_lane = lax.broadcasted_iota(jnp.int32, (8, slots), 1)
        slot_lane = jnp.where(slot_lane < peers, slot_lane * CAP, (slot_lane - peers) * CAP + 1)

        def name_slots(j, carry):
            for k in range(cands):
                rows = pl.ds(pl.multiple_of((k * own_rows + j) * 8, 8), 8)
                named[rows, :] = jnp.where(slot_lane == buckets[step, k, j], 1.0, 0.0)
            return carry

        lax.fori_loop(0, own_rows, name_slots, 0)
        slot_hot = jnp.transpose(named[...]).astype(BF16)

        everything = pl.ds(0, slots - CAP)
        whole = pltpu.make_async_remote_copy(
            src_ref=send_geo.at[everything],
            dst_ref=recv_geo.at[step, everything],
            send_sem=geo_sem.at[0, step],
            recv_sem=geo_sem.at[1, step],
            device_id=mesh_next,
            device_id_type=MESH,
        )
        whole.wait_recv()

        def quadratics(j, both):
            for k in range(cands):
                block = recv_geo[step, buckets[step, k, j]]
                centre, normal = block[:3], block[3:6]
                along = jnp.sum(centre * normal, axis=0, keepdims=True)
                square = jnp.sum(centre * centre, axis=0, keepdims=True)
                nothing = jnp.zeros((1, SEG), F32)
                blank = jnp.zeros((3, SEG), F32)
                depth = jnp.concatenate([-normal, nothing, along, blank], axis=0) * ROOT_SCALE
                far = jnp.concatenate([-2.0 * centre, nothing + 1.0, square, blank], axis=0)
                top, mid, low = thirds(jnp.concatenate([depth, far * EXP2_SCALE], axis=1))
                pieces = jnp.concatenate([top, mid, top, mid, low, top], axis=0).astype(BF16)
                at = slice(k * 2 * SEG, (k + 1) * 2 * SEG)
                both[:, at] = jnp.dot(pcol[j], pieces, preferred_element_type=F32)

        def contact(j, both, wtop, wlow, normals_at):
            normals = []
            for k in range(cands):
                normals.append(recv_geo[step, buckets[step, k, j]][3:6])
                total = jnp.zeros((8, SEG), F32)
                for part in range(SEG // 16):
                    at = slice(part * 16, part * 16 + 16)
                    depth = both[at, k * 2 * SEG : (k * 2 + 1) * SEG]
                    far = both[at, (k * 2 + 1) * SEG : (k * 2 + 2) * SEG]
                    weight = (
                        jnp.maximum(depth, 0.0) * jnp.exp2(depth * depth - far) * mcol[k, j, at, :]
                    )
                    total = total + weight[:8] + weight[8:]
                    top, low = halves(weight)
                    wtop[at, k * SEG : (k + 1) * SEG] = top
                    wlow[at, k * SEG : (k + 1) * SEG] = low
                wsum[pl.ds(pl.multiple_of((k * own_rows + j) * 8, 8), 8), :] = total
            zeros = jnp.zeros((5, cands * SEG), F32)
            flat = jnp.concatenate([jnp.concatenate(normals, axis=1), zeros], axis=0)
            top = flat.astype(BF16).astype(F32)
            normals_at[...] = jnp.concatenate([top, flat - top], axis=0).astype(BF16)

        def push(j, wtop, wlow, normals_at):
            both = normals_at[...]
            force = dot_nt(both, wtop[...])
            rest = dot_nt(both, wlow[...])
            force = force[:8] + force[8:] + rest[:8]
            for c in range(3):
                slave[c, pl.ds(j, 1), :] = force[c : c + 1]

        even = (wtop_a, wlow_a, normals_a)
        odd = (wtop_b, wlow_b, normals_b)

        def contact_pair(half, carry):
            quadratics(2 * half + 1, pairs_b)
            push(jnp.maximum(2 * half - 1, 0), *odd)
            contact(2 * half, pairs_a, *even)
            quadratics(jnp.minimum(2 * half + 2, own_rows - 1), pairs_a)
            push(2 * half, *even)
            contact(2 * half + 1, pairs_b, *odd)
            return carry

        quadratics(0, pairs_a)

        lax.fori_loop(0, own_rows // 2, contact_pair, 0)
        push(own_rows - 1, *odd)

        top, low = halves(wsum[...])
        slot_sum = jnp.dot(slot_hot, top, preferred_element_type=F32) + jnp.dot(
            slot_hot, low, preferred_element_type=F32
        )
        for c in range(CAP):
            ret_send[step, :, c, :] = slot_sum[c * peers : (c + 1) * peers]

        def return_copy(peer):
            return pltpu.make_async_remote_copy(
                src_ref=ret_send.at[step, peer],
                dst_ref=ret_recv.at[step, me],
                send_sem=ret_sem.at[0, step],
                recv_sem=ret_sem.at[1, step],
                device_id=(peer, my_sub),
                device_id_type=MESH,
            )

        each_partner(lambda peer: return_copy(peer).start())
        ret_recv[step, me] = ret_send[step, me]
        pick_hot = lax.broadcasted_iota(jnp.int32, (blocks, slots), 0)
        order = lax.broadcasted_iota(jnp.int32, (8, slots), 1)
        order = jnp.where(order < peers, order * CAP, (order - peers) * CAP + 1)
        picked = jnp.broadcast_to(pick_rows[pl.ds(step, 1), :], (8, slots))
        picked = jnp.take_along_axis(picked, order, axis=1, mode="promise_in_bounds")
        pick_hot = jnp.where(pick_hot == picked[:1], 1.0, 0.0).astype(BF16)
        others = pl.ds(0, peers - 1)
        back = pltpu.make_async_remote_copy(
            src_ref=ret_send.at[step, others],
            dst_ref=ret_recv.at[step, others],
            send_sem=ret_sem.at[0, step],
            recv_sem=ret_sem.at[1, step],
            device_id=mesh_next,
            device_id_type=MESH,
        )
        back.wait_recv()
        returned = jnp.concatenate([ret_recv[step, :, c, :] for c in range(CAP)], axis=0)
        top, low = halves(returned)
        press = jnp.dot(pick_hot, top, preferred_element_type=F32) + jnp.dot(
            pick_hot, low, preferred_element_type=F32
        )
        for c in range(3):
            store_halves(0, c, slice(None), -0.25 * nrm[c] * press)
        react = scatter(1)
        force = [node_force[c] + react[c] for c in range(6)]
        for c in range(3):
            f_send_m[step, c] = force[3 + c][:GHOST_ROWS]
            f_send_s[step, c] = force[3 + c][GHOST_ROWS:]
        back_copies = step_copies(step)
        for copy in back_copies[:4]:
            copy.start()
        for c in range(3):
            part[c] = force[c] + slave[c]
        shared = take(part, own_rows, sids[...])
        for c in range(3):
            o_send_m[step, c] = shared[c][:GHOST_ROWS]
            o_send_s[step, c] = shared[c][GHOST_ROWS:]
        for copy in back_copies[4:]:
            copy.start()
        for copy in back_copies:
            copy.wait()

        def ghost_sum(values, hot, from_mesh, from_sub):
            for c in range(3):
                for r in range(GHOST_ROWS):
                    values[c : c + 1, r * SEG : (r + 1) * SEG] = from_mesh[step, c, r : r + 1]
                    at = (GHOST_ROWS + r) * SEG
                    values[c : c + 1, at : at + SEG] = from_sub[step, c, r : r + 1]
            top = values[...].astype(BF16).astype(F32)
            both = jnp.concatenate([top, values[...] - top], axis=0).astype(BF16)
            total = dot_nt(both, hot[...])
            return total[:8] + total[8:]

        sum_m = ghost_sum(values_m, same_m, f_send_m, x_recv_s)
        sum_s = ghost_sum(values_s, same_s, x_recv_m, f_send_s)
        for c in range(3):
            rows = [sum_m[c : c + 1, r * SEG : (r + 1) * SEG] for r in range(GHOST_ROWS)]
            rows += [sum_s[c : c + 1, r * SEG : (r + 1) * SEG] for r in range(GHOST_ROWS)]
            owned = jnp.concatenate([o_recv_m[step, c], o_recv_s[step, c]], axis=0)
            total = owned + jnp.concatenate(rows, axis=0)
            vel[c, own_rows:, :] = vel[c, own_rows:, :] + TIME_STEP * total / ghost_mass
        terms = []
        for c in range(3):
            came = jnp.concatenate([f_recv_m[step, c], f_recv_s[step, c]], axis=0)
            tops, lows = [], []
            for r in range(2 * GHOST_ROWS):
                high = lax.shift_right_logical(sids[r : r + 1, :], 7)
                top, low = halves(jnp.where(high_lane == high, came[r : r + 1], 0.0))
                tops.append(top)
                lows.append(low)
            terms.append(jnp.concatenate(tops, axis=1))
            terms.append(jnp.concatenate(lows, axis=1))
        added = dot_nt(jnp.concatenate(terms, axis=0), onehot_back[...])
        for c in range(3):
            own = part[c] + added[c * 32 : c * 32 + own_rows] + added[c * 32 + 16 : c * 32 + 16 + own_rows]
            now = vel[c, :own_rows, :] + TIME_STEP * own / mass[0]
            vel[c, :own_rows, :] = now
            pos[c] = pos[c] + TIME_STEP * now
        whole.wait_send()
        back.wait_send()

        return step_carry

    lax.fori_loop(0, STEPS, one_step, 0)

    def velocity_lanes(row, carry):
        for c in range(3):
            vel_out[pl.ds(c, 1), lanes_of(row)] = vel[c, pl.ds(row, 1), :]
        return carry

    def stress_lanes(row, carry):
        for c in range(3):
            stress_out[pl.ds(c, 1), lanes_of(row)] = snow[c, pl.ds(row, 1), :]
        return carry

    lax.fori_loop(0, own_rows, velocity_lanes, 0)
    lax.fori_loop(0, blocks, stress_lanes, 0)


def per_device(
    coords, veloc, node_mass, stress, connect, send_mesh, send_sub, send_pick, bucket_list, pair_mask
):
    peers = lax.axis_size("mesh")
    nodes = coords.shape[1]
    elems = stress.shape[1]
    own_rows, blocks = nodes // SEG, elems // SEG
    cands = bucket_list.shape[1]
    slots = send_pick.shape[1]
    pairs = cands * own_rows
    table_rows = own_rows + 2 * GHOST_ROWS
    in_vmem = pl.BlockSpec(memory_space=pltpu.VMEM)
    in_smem = pl.BlockSpec(memory_space=pltpu.SMEM)
    v = pltpu.VMEM
    return pl.pallas_call(
        functools.partial(kernel, own_rows, blocks, cands),
        out_shape=(
            jax.ShapeDtypeStruct((3, nodes), F32),
            jax.ShapeDtypeStruct((3, elems), F32),
        ),
        in_specs=[in_vmem] * 7 + [in_smem] * 2 + [in_vmem] * 2,
        out_specs=(in_vmem, in_vmem),
        scratch_shapes=[
            v((4, blocks, SEG), jnp.int32),
            v((2 * GHOST_ROWS, SEG), jnp.int32),
            v((3, own_rows, SEG), F32),
            v((3, table_rows, SEG), F32),
            v((1, own_rows, SEG), F32),
            v((4, 3, blocks, SEG), F32),
            v((4, 3, blocks, SEG), F32),
            v((3, blocks, SEG), F32),
            v((3, blocks, SEG), F32),
            v((blocks, SEG), F32),
            v((blocks, 6, SEG), F32),
            v((slots, 6, SEG), F32),
            v((STEPS, slots, 6, SEG), F32),
            v((SEG, 4 * elems), BF16),
            v((SEG, 2 * GHOST_ROWS * SEG), BF16),
            v((32, 4 * elems), BF16),
            *[v((144, 32 * SEG), BF16)] * 2,
            v((4, 3, blocks, SEG), F32),
            v((4, 3, blocks, SEG), F32),
            v((3, table_rows, SEG), F32),
            v((own_rows, SEG, 48), BF16),
            v((cands, own_rows, SEG, SEG), F32),
            v((SEG, cands * 2 * SEG), F32),
            v((SEG, cands * 2 * SEG), F32),
            v((SEG, cands * SEG), BF16),
            v((SEG, cands * SEG), BF16),
            v((16, cands * SEG), BF16),
            v((SEG, cands * SEG), BF16),
            v((SEG, cands * SEG), BF16),
            v((16, cands * SEG), BF16),
            v((pairs * 8, SEG), F32),
            v((pairs * 8, slots), F32),
            v((3, own_rows, SEG), F32),
            v((STEPS, peers, CAP, SEG), F32),
            v((STEPS, peers, CAP, SEG), F32),
            *[v((7, GHOST_ROWS, SEG), F32)] * 4,
            *[v((2 * GHOST_ROWS, SEG), jnp.int32)] * 2,
            *[v((GHOST_ROWS * SEG, 2 * GHOST_ROWS * SEG), BF16)] * 2,
            *[v((8, 2 * GHOST_ROWS * SEG), F32)] * 2,
            v((3, own_rows, SEG), F32),
            *[v((STEPS, 3, GHOST_ROWS, SEG), F32)] * 10,
            pltpu.SemaphoreType.DMA((8 + STEPS * 12,)),
            pltpu.SemaphoreType.DMA((2, STEPS)),
            pltpu.SemaphoreType.DMA((2, STEPS)),
        ],
        compiler_params=pltpu.CompilerParams(
            collective_id=0, has_side_effects=True, vmem_limit_bytes=56 * 1024 * 1024
        ),
    )(
        coords,
        veloc,
        node_mass.reshape(1, nodes),
        stress,
        connect,
        send_mesh.reshape(1, -1),
        send_sub.reshape(1, -1),
        send_pick,
        bucket_list,
        send_pick,
        pair_mask,
    )


def solution(mesh):
    both = ("mesh", "sub")
    return jax.shard_map(
        per_device,
        mesh=mesh,
        in_specs=(
            P(None, both),
            P(None, both),
            P(both),
            P(None, both),
            P(None, both),
            P(both),
            P(both),
            P(None, both),
            P(None, None, both),
            P(None, None, both),
        ),
        out_specs=(P(None, both), P(None, both)),
        check_vma=False,
    )
```

```python
import functools
import math

import jax
import jax.numpy as jnp
from jax import lax
from jax.experimental import pallas as pl
from jax.experimental.pallas import tpu as pltpu
from jax.sharding import PartitionSpec as P

SEG = 128
STEPS = 4
CAP = 2
TIME_STEP = 0.2
YOUNG = 1.0
POISSON = 0.3
HOURGLASS = 0.01
PENALTY = 0.2
REACH = 4.0
PLANE_STIFF = YOUNG / (1.0 - POISSON * POISSON)
SHEAR_STIFF = YOUNG / (2.0 * (1.0 + POISSON))
EXP2_SCALE = math.log2(math.e) / REACH
ROOT_SCALE = math.sqrt(EXP2_SCALE)
MESH = pl.DeviceIdType.MESH
F32 = jnp.float32
BF16 = jnp.bfloat16
NT = (((1,), (1,)), ((), ()))
GHOST_ROWS = 4


def dot_nt(lhs, rhs):
    return lax.dot_general(lhs, rhs, NT, preferred_element_type=F32)


def halves(value):
    top = value.astype(BF16)
    return top, (value - top.astype(F32)).astype(BF16)


def thirds(value):
    top = value.astype(BF16).astype(F32)
    rest = value - top
    mid = rest.astype(BF16).astype(F32)
    return top, mid, rest - mid


def cross(u, v):
    return (
        u[1] * v[2] - u[2] * v[1],
        u[2] * v[0] - u[0] * v[2],
        u[0] * v[1] - u[1] * v[0],
    )


def dot3(u, v):
    return u[0] * v[0] + u[1] * v[1] + u[2] * v[2]


def kernel(
    own_rows,
    blocks,
    cands,
    coords,
    veloc,
    mass_in,
    stress_in,
    connect,
    send_mesh,
    send_sub,
    picks,
    buckets,
    pick_rows,
    pair_mask,
    vel_out,
    stress_out,
    ids,
    sids,
    pos,
    vel,
    mass,
    cpos,
    cvel,
    snow,
    nrm,
    area,
    geo,
    send_geo,
    recv_geo,
    onehot,
    onehot_back,
    rowhot,
    spread_a,
    spread_b,
    ftop,
    flow,
    table,
    pcol,
    mcol,
    pairs_a,
    pairs_b,
    wtop_a,
    wlow_a,
    normals_a,
    wtop_b,
    wlow_b,
    normals_b,
    wsum,
    named,
    slave,
    ret_send,
    ret_recv,
    first_send_m,
    first_send_s,
    first_recv_m,
    first_recv_s,
    sids_m,
    sids_s,
    same_m,
    same_s,
    values_m,
    values_s,
    part,
    o_send_m,
    o_send_s,
    o_recv_m,
    o_recv_s,
    f_send_m,
    f_send_s,
    f_recv_m,
    f_recv_s,
    x_recv_m,
    x_recv_s,
    halo_sem,
    geo_sem,
    ret_sem,
):
    peers = lax.axis_size("mesh")
    subs = lax.axis_size("sub")
    me = lax.axis_index("mesh")
    my_sub = lax.axis_index("sub")
    mesh_next = (lax.rem(me + 1, peers), my_sub)
    mesh_prev = (lax.rem(me + peers - 1, peers), my_sub)
    sub_next = (me, lax.rem(my_sub + 1, subs))
    sub_prev = (me, lax.rem(my_sub + subs - 1, subs))
    corner_a = (mesh_prev[0], sub_next[1])
    corner_b = (mesh_next[0], sub_prev[1])
    slots = peers * CAP
    chunks = blocks // 8
    pairs = cands * own_rows

    ring_x, ring_z = 4, peers // 8
    my_core, my_z, my_x = me % 2, me // 2 % ring_z, me // (2 * ring_z)

    def spread_out(ring, turn):
        return ring // 2 + (turn + 1) // 2 * (1 - 2 * (turn % 2))

    def each_partner(act):
        def one_x(turn, carry):
            x = lax.rem(my_x + spread_out(ring_x, turn), ring_x)
            for turn_z in range(ring_z):
                z = lax.rem(my_z + spread_out(ring_z, turn_z), ring_z)
                chip = (x * ring_z + z) * 2
                act(chip + 1 - my_core)
                if turn_z < ring_z - 1:
                    act(chip + my_core)
                else:
                    pl.when(turn < ring_x - 1)(lambda chip=chip: act(chip + my_core))
            return carry

        lax.fori_loop(0, ring_x, one_x, 0)

    barrier = pltpu.get_barrier_semaphore()

    def greet(hop, carry):
        pl.semaphore_signal(
            barrier, inc=1, device_id=(lax.rem(me + hop, peers), my_sub), device_id_type=MESH
        )
        return carry

    lax.fori_loop(1, peers, greet, 0)
    for other in (sub_next, sub_prev, corner_a, corner_b):
        pl.semaphore_signal(barrier, inc=1, device_id=other, device_id_type=MESH)

    def lanes_of(row):
        return pl.ds(pl.multiple_of(row * SEG, SEG), SEG)

    def rows_of_nodes(row, carry):
        for c in range(3):
            pos[c, pl.ds(row, 1), :] = coords[pl.ds(c, 1), lanes_of(row)]
            vel[c, pl.ds(row, 1), :] = veloc[pl.ds(c, 1), lanes_of(row)]
        mass[0, pl.ds(row, 1), :] = mass_in[:, lanes_of(row)]
        return carry

    def rows_of_elems(row, carry):
        for c in range(3):
            snow[c, pl.ds(row, 1), :] = stress_in[pl.ds(c, 1), lanes_of(row)]
        for i in range(4):
            ids[i, pl.ds(row, 1), :] = connect[pl.ds(i, 1), lanes_of(row)]
        return carry

    lax.fori_loop(0, own_rows, rows_of_nodes, 0)
    for r in range(GHOST_ROWS):
        sids[r : r + 1, :] = send_mesh[:, r * SEG : (r + 1) * SEG]
        sids[GHOST_ROWS + r : GHOST_ROWS + r + 1, :] = send_sub[:, r * SEG : (r + 1) * SEG]

    def take(tables, rows, index, comps=3):
        low = lax.bitwise_and(index, SEG - 1)
        high = lax.shift_right_logical(index, 7)
        found = [jnp.zeros(index.shape, F32) for _ in range(comps)]
        for r in range(rows):
            here = high == r
            for c in range(comps):
                source = jnp.broadcast_to(tables[c, r : r + 1, :], index.shape)
                got = jnp.take_along_axis(source, low, axis=1, mode="promise_in_bounds")
                found[c] = jnp.where(here, got, found[c])
        return found

    def halo_copy(src, dst, slot, target):
        return pltpu.make_async_remote_copy(
            src_ref=src,
            dst_ref=dst,
            send_sem=halo_sem.at[slot],
            recv_sem=halo_sem.at[slot + 1],
            device_id=target,
            device_id_type=MESH,
        )

    first_copies = (
        halo_copy(first_send_m, first_recv_m, 0, mesh_next),
        halo_copy(first_send_s, first_recv_s, 2, sub_next),
        halo_copy(sids, sids_m, 4, mesh_next),
        halo_copy(sids, sids_s, 6, sub_next),
    )

    def step_copies(step):
        base = 8 + step * 12
        return (
            halo_copy(f_send_m.at[step], x_recv_m.at[step], base, corner_a),
            halo_copy(f_send_s.at[step], x_recv_s.at[step], base + 2, corner_b),
            halo_copy(f_send_m.at[step], f_recv_m.at[step], base + 4, mesh_prev),
            halo_copy(f_send_s.at[step], f_recv_s.at[step], base + 6, sub_prev),
            halo_copy(o_send_m.at[step], o_recv_m.at[step], base + 8, mesh_next),
            halo_copy(o_send_s.at[step], o_recv_s.at[step], base + 10, sub_next),
        )

    firsts = take(pos, own_rows, sids[...]) + take(vel, own_rows, sids[...])
    for q, got in enumerate(firsts + take(mass, own_rows, sids[...], 1)):
        first_send_m[q] = got[:GHOST_ROWS]
        first_send_s[q] = got[GHOST_ROWS:]

    lax.fori_loop(0, blocks, rows_of_elems, 0)
    for ref in (wtop_b, wlow_b, normals_b):
        ref[...] = jnp.zeros(ref.shape, BF16)
    for ref in (values_m, values_s):
        ref[...] = jnp.zeros(ref.shape, F32)

    pl.semaphore_wait(barrier, peers + 3)
    for copy in first_copies:
        copy.start()

    high_lane = lax.broadcasted_iota(jnp.int32, (16, SEG), 0)
    ghost_lane = lax.bitwise_and(high_lane, 7) + own_rows

    def make_onehot(row, carry):
        lane = lax.broadcasted_iota(jnp.int32, (SEG, SEG), 0)
        for i in range(4):
            index = ids[i, pl.ds(row, 1), :]
            low = lax.bitwise_and(index, SEG - 1)
            high = lax.shift_right_logical(index, 7)
            cols = pl.ds(pl.multiple_of((row * 4 + i) * SEG, SEG), SEG)
            onehot[:, cols] = jnp.where(lane == low, 1.0, 0.0).astype(BF16)
            rowhot[:16, cols] = jnp.where(high_lane == high, 1.0, 0.0).astype(BF16)
            rowhot[16:, cols] = jnp.where(ghost_lane == high, 1.0, 0.0).astype(BF16)
        return carry

    lax.fori_loop(0, blocks, make_onehot, 0)
    for r in range(2 * GHOST_ROWS):
        lane = lax.broadcasted_iota(jnp.int32, (SEG, SEG), 0)
        low = lax.bitwise_and(sids[r : r + 1, :], SEG - 1)
        onehot_back[:, r * SEG : (r + 1) * SEG] = jnp.where(lane == low, 1.0, 0.0).astype(BF16)

    for copy in first_copies:
        copy.wait()
    for c in range(3):
        table[c, :own_rows, :] = pos[c]
        for got, at in ((first_recv_m, own_rows), (first_recv_s, own_rows + GHOST_ROWS)):
            table[c, at : at + GHOST_ROWS, :] = got[c]
            vel[c, at : at + GHOST_ROWS, :] = got[3 + c]
    ghost_mass = jnp.concatenate([first_recv_m[6], first_recv_s[6]], axis=0)

    def match(hot, lists, first):
        names = lists[...].astype(F32)
        for q in range(GHOST_ROWS):
            mine = names[first + q : first + q + 1]
            mine = jnp.transpose(jnp.broadcast_to(mine, (SEG, SEG)))
            for r in range(2 * GHOST_ROWS):
                same = jnp.where(mine == names[r : r + 1], 1.0, 0.0)
                hot[q * SEG : (q + 1) * SEG, r * SEG : (r + 1) * SEG] = same.astype(BF16)

    match(same_m, sids_m, 0)
    match(same_s, sids_s, GHOST_ROWS)

    def first_positions(part, carry):
        rows = pl.ds(pl.multiple_of(part * 8, 8), 8)
        for i in range(4):
            got = take(table, own_rows + 2 * GHOST_ROWS, ids[i, rows, :])
            for c in range(3):
                cpos[i, c, rows, :] = got[c]
        return carry

    lax.fori_loop(0, chunks, first_positions, 0)

    def scatter(corners):
        def build(part, spread):
            for r in range(8):
                row = part * 8 + r
                values = []
                for i in range(corners):
                    for c in range(3):
                        top = ftop[i, c, pl.ds(row, 1), :]
                        low = flow[i, c, pl.ds(row, 1), :]
                        top8 = jnp.broadcast_to(top, (8, SEG))
                        low8 = jnp.broadcast_to(low, (8, SEG))
                        values.append(
                            (
                                jnp.concatenate([top8, top8], axis=0).astype(BF16),
                                jnp.concatenate([low8, low8], axis=0).astype(BF16),
                                jnp.concatenate([top8, low8], axis=0).astype(BF16),
                            )
                        )
                for i in range(4):
                    cols = pl.ds(pl.multiple_of((row * 4 + i) * SEG, SEG), SEG)
                    at = slice((r * 4 + i) * SEG, (r * 4 + i + 1) * SEG)
                    here = rowhot[:16, cols]
                    away = rowhot[16:, cols]
                    for c in range(3):
                        top, low, both = values[(i if corners > 1 else 0) * 3 + c]
                        spread[c * 32 : c * 32 + 16, at] = here * top
                        spread[c * 32 + 16 : c * 32 + 32, at] = here * low
                        spread[96 + c * 16 : 112 + c * 16, at] = away * both

        def product(part, spread):
            cols = pl.ds(pl.multiple_of(part * 32 * SEG, 32 * SEG), 32 * SEG)
            return dot_nt(spread[...], onehot[:, cols])

        def two_parts(half, carry):
            build(2 * half + 1, spread_b)
            carry = carry + product(2 * half, spread_a)
            build(jnp.minimum(2 * half + 2, chunks - 1), spread_a)
            return carry + product(2 * half + 1, spread_b)

        build(0, spread_a)
        total = lax.fori_loop(0, chunks // 2, two_parts, jnp.zeros((144, SEG), F32))
        own = [total[c * 32 : c * 32 + 16] + total[c * 32 + 16 : c * 32 + 32] for c in range(3)]
        ghost = [
            total[96 + c * 16 : 104 + c * 16] + total[104 + c * 16 : 112 + c * 16] for c in range(3)
        ]
        return own + ghost

    def store_halves(i, c, rows, value):
        top = value.astype(BF16).astype(F32)
        ftop[i, c, rows, :] = top
        flow[i, c, rows, :] = value - top

    def one_step(step, step_carry):
        advance = jnp.where(step > 0, TIME_STEP, 0.0).astype(F32)

        def shapes(part, carry):
            rows = pl.ds(pl.multiple_of(part * 8, 8), 8)
            a = []
            for i in range(4):
                w = take(vel, own_rows + 2 * GHOST_ROWS, ids[i, rows, :])
                at = []
                for c in range(3):
                    cvel[i, c, rows, :] = w[c]
                    moved = cpos[i, c, rows, :] + advance * w[c]
                    cpos[i, c, rows, :] = moved
                    at.append(moved)
                a.append(at)
            raw = cross(
                [a[2][c] - a[0][c] for c in range(3)], [a[3][c] - a[1][c] for c in range(3)]
            )
            twice = jnp.maximum(jnp.sqrt(dot3(raw, raw)), 1.0)
            area[rows, :] = twice
            for c in range(3):
                n = raw[c] / twice
                centre = 0.25 * (a[0][c] + a[1][c] + a[2][c] + a[3][c])
                nrm[c, rows, :] = n
                geo[rows, c, :] = centre
                geo[rows, 3 + c, :] = n
            return carry

        lax.fori_loop(0, chunks, shapes, 0)

        def block_copy(peer):
            return pltpu.make_async_remote_copy(
                src_ref=send_geo.at[pl.ds(peer * CAP, CAP)],
                dst_ref=recv_geo.at[step, pl.ds(me * CAP, CAP)],
                send_sem=geo_sem.at[0, step],
                recv_sem=geo_sem.at[1, step],
                device_id=(peer, my_sub),
                device_id_type=MESH,
            )

        def send_blocks(peer):
            for c in range(CAP):
                send_geo[peer * CAP + c] = geo[picks[step, peer * CAP + c]]
            block_copy(peer).start()

        each_partner(send_blocks)
        for c in range(CAP):
            recv_geo[step, me * CAP + c] = geo[picks[step, me * CAP + c]]

        def inner_forces(part, carry):
            rows = pl.ds(pl.multiple_of(part * 8, 8), 8)
            a = [[cpos[i, c, rows, :] for c in range(3)] for i in range(4)]
            w = [[cvel[i, c, rows, :] for c in range(3)] for i in range(4)]
            n = [nrm[c, rows, :] for c in range(3)]
            twice = area[rows, :]
            centre = [geo[rows, c, :] for c in range(3)]
            side = [a[1][c] - a[0][c] for c in range(3)]
            length = jnp.maximum(jnp.sqrt(dot3(side, side)), 1.0)
            one = [side[c] / length for c in range(3)]
            two = cross(n, one)
            rel = [[a[i][c] - centre[c] for c in range(3)] for i in range(4)]
            x = [dot3(rel[i], one) for i in range(4)]
            y = [dot3(rel[i], two) for i in range(4)]
            u = [dot3(w[i], one) for i in range(4)]
            v = [dot3(w[i], two) for i in range(4)]
            inverse = 1.0 / twice
            b20, b31 = (y[2] - y[0]) * inverse, (y[1] - y[3]) * inverse
            bx = [b31, b20, -b31, -b20]
            c02, c31 = (x[0] - x[2]) * inverse, (x[3] - x[1]) * inverse
            by = [c31, c02, -c31, -c02]
            exx = b31 * (u[0] - u[2]) + b20 * (u[1] - u[3])
            eyy = c31 * (v[0] - v[2]) + c02 * (v[1] - v[3])
            exy = (
                c31 * (u[0] - u[2]) + c02 * (u[1] - u[3]) + b31 * (v[0] - v[2]) + b20 * (v[1] - v[3])
            )
            s0 = snow[0, rows, :] + TIME_STEP * (PLANE_STIFF * (exx + POISSON * eyy))
            s1 = snow[1, rows, :] + TIME_STEP * (PLANE_STIFF * (POISSON * exx + eyy))
            s2 = snow[2, rows, :] + TIME_STEP * (SHEAR_STIFF * exy)
            snow[0, rows, :] = s0
            snow[1, rows, :] = s1
            snow[2, rows, :] = s2
            half = 0.5 * twice
            hx = x[0] - x[1] + x[2] - x[3]
            hy = y[0] - y[1] + y[2] - y[3]
            signs = (1.0, -1.0, 1.0, -1.0)
            g = [signs[i] - hx * bx[i] - hy * by[i] for i in range(4)]
            r = [
                HOURGLASS * (g[0] * w[0][c] + g[1] * w[1][c] + g[2] * w[2][c] + g[3] * w[3][c])
                for c in range(3)
            ]
            for i in range(4):
                fx = half * (bx[i] * s0 + by[i] * s2)
                fy = half * (by[i] * s1 + bx[i] * s2)
                for c in range(3):
                    store_halves(i, c, rows, -(fx * one[c] + fy * two[c] + g[i] * r[c]))
            return carry

        lax.fori_loop(0, chunks, inner_forces, 0)
        node_force = scatter(4)

        def columns(j, carry):
            p = [pos[c, pl.ds(j, 1), :] for c in range(3)]
            one = jnp.ones((1, SEG), F32)
            top, mid, low = thirds(
                jnp.concatenate(p + [dot3(p, p), one, jnp.zeros((3, SEG), F32)], axis=0)
            )
            pieces = jnp.concatenate([top, top, mid, mid, top, low], axis=0)
            pcol[j] = jnp.transpose(pieces).astype(BF16)
            for k in range(cands):
                row = pair_mask[step, pl.ds(k, 1), lanes_of(j)].astype(F32) * (PENALTY / ROOT_SCALE)
                mcol[k, j] = jnp.transpose(jnp.broadcast_to(row, (SEG, SEG)))
            return carry

        lax.fori_loop(0, own_rows, columns, 0)

        slot_lane = lax.broadcasted_iota(jnp.int32, (8, slots), 1)
        slot_lane = jnp.where(slot_lane < peers, slot_lane * CAP, (slot_lane - peers) * CAP + 1)

        def name_slots(j, carry):
            for k in range(cands):
                rows = pl.ds(pl.multiple_of((k * own_rows + j) * 8, 8), 8)
                named[rows, :] = jnp.where(slot_lane == buckets[step, k, j], 1.0, 0.0)
            return carry

        lax.fori_loop(0, own_rows, name_slots, 0)
        slot_hot = jnp.transpose(named[...]).astype(BF16)

        everything = pl.ds(0, slots - CAP)
        whole = pltpu.make_async_remote_copy(
            src_ref=send_geo.at[everything],
            dst_ref=recv_geo.at[step, everything],
            send_sem=geo_sem.at[0, step],
            recv_sem=geo_sem.at[1, step],
            device_id=mesh_next,
            device_id_type=MESH,
        )
        whole.wait_recv()

        def quadratics(j, both):
            for k in range(cands):
                block = recv_geo[step, buckets[step, k, j]]
                centre, normal = block[:3], block[3:6]
                along = jnp.sum(centre * normal, axis=0, keepdims=True)
                square = jnp.sum(centre * centre, axis=0, keepdims=True)
                nothing = jnp.zeros((1, SEG), F32)
                blank = jnp.zeros((3, SEG), F32)
                depth = jnp.concatenate([-normal, nothing, along, blank], axis=0) * ROOT_SCALE
                far = jnp.concatenate([-2.0 * centre, nothing + 1.0, square, blank], axis=0)
                top, mid, low = thirds(jnp.concatenate([depth, far * EXP2_SCALE], axis=1))
                pieces = jnp.concatenate([top, mid, top, mid, low, top], axis=0).astype(BF16)
                at = slice(k * 2 * SEG, (k + 1) * 2 * SEG)
                both[:, at] = jnp.dot(pcol[j], pieces, preferred_element_type=F32)

        def contact(j, both, wtop, wlow, normals_at):
            normals = []
            for k in range(cands):
                normals.append(recv_geo[step, buckets[step, k, j]][3:6])
                total = jnp.zeros((8, SEG), F32)
                for part in range(SEG // 16):
                    at = slice(part * 16, part * 16 + 16)
                    depth = both[at, k * 2 * SEG : (k * 2 + 1) * SEG]
                    far = both[at, (k * 2 + 1) * SEG : (k * 2 + 2) * SEG]
                    weight = (
                        jnp.maximum(depth, 0.0) * jnp.exp2(depth * depth - far) * mcol[k, j, at, :]
                    )
                    total = total + weight[:8] + weight[8:]
                    top, low = halves(weight)
                    wtop[at, k * SEG : (k + 1) * SEG] = top
                    wlow[at, k * SEG : (k + 1) * SEG] = low
                wsum[pl.ds(pl.multiple_of((k * own_rows + j) * 8, 8), 8), :] = total
            zeros = jnp.zeros((5, cands * SEG), F32)
            flat = jnp.concatenate([jnp.concatenate(normals, axis=1), zeros], axis=0)
            top = flat.astype(BF16).astype(F32)
            normals_at[...] = jnp.concatenate([top, flat - top], axis=0).astype(BF16)

        def push(j, wtop, wlow, normals_at):
            both = normals_at[...]
            force = dot_nt(both, wtop[...])
            rest = dot_nt(both, wlow[...])
            force = force[:8] + force[8:] + rest[:8]
            for c in range(3):
                slave[c, pl.ds(j, 1), :] = force[c : c + 1]

        even = (wtop_a, wlow_a, normals_a)
        odd = (wtop_b, wlow_b, normals_b)

        def contact_pair(half, carry):
            quadratics(2 * half + 1, pairs_b)
            push(jnp.maximum(2 * half - 1, 0), *odd)
            contact(2 * half, pairs_a, *even)
            quadratics(jnp.minimum(2 * half + 2, own_rows - 1), pairs_a)
            push(2 * half, *even)
            contact(2 * half + 1, pairs_b, *odd)
            return carry

        quadratics(0, pairs_a)

        lax.fori_loop(0, own_rows // 2, contact_pair, 0)
        push(own_rows - 1, *odd)

        top, low = halves(wsum[...])
        slot_sum = jnp.dot(slot_hot, top, preferred_element_type=F32) + jnp.dot(
            slot_hot, low, preferred_element_type=F32
        )
        for c in range(CAP):
            ret_send[step, :, c, :] = slot_sum[c * peers : (c + 1) * peers]

        def return_copy(peer):
            return pltpu.make_async_remote_copy(
                src_ref=ret_send.at[step, peer],
                dst_ref=ret_recv.at[step, me],
                send_sem=ret_sem.at[0, step],
                recv_sem=ret_sem.at[1, step],
                device_id=(peer, my_sub),
                device_id_type=MESH,
            )

        each_partner(lambda peer: return_copy(peer).start())
        ret_recv[step, me] = ret_send[step, me]
        pick_hot = lax.broadcasted_iota(jnp.int32, (blocks, slots), 0)
        order = lax.broadcasted_iota(jnp.int32, (8, slots), 1)
        order = jnp.where(order < peers, order * CAP, (order - peers) * CAP + 1)
        picked = jnp.broadcast_to(pick_rows[pl.ds(step, 1), :], (8, slots))
        picked = jnp.take_along_axis(picked, order, axis=1, mode="promise_in_bounds")
        pick_hot = jnp.where(pick_hot == picked[:1], 1.0, 0.0).astype(BF16)
        others = pl.ds(0, peers - 1)
        back = pltpu.make_async_remote_copy(
            src_ref=ret_send.at[step, others],
            dst_ref=ret_recv.at[step, others],
            send_sem=ret_sem.at[0, step],
            recv_sem=ret_sem.at[1, step],
            device_id=mesh_next,
            device_id_type=MESH,
        )
        back.wait_recv()
        returned = jnp.concatenate([ret_recv[step, :, c, :] for c in range(CAP)], axis=0)
        top, low = halves(returned)
        press = jnp.dot(pick_hot, top, preferred_element_type=F32) + jnp.dot(
            pick_hot, low, preferred_element_type=F32
        )
        for c in range(3):
            store_halves(0, c, slice(None), -0.25 * nrm[c] * press)
        react = scatter(1)
        force = [node_force[c] + react[c] for c in range(6)]
        for c in range(3):
            f_send_m[step, c] = force[3 + c][:GHOST_ROWS]
            f_send_s[step, c] = force[3 + c][GHOST_ROWS:]
        back_copies = step_copies(step)
        for copy in back_copies[2:4]:
            copy.start()
        for c in range(3):
            part[c] = force[c] + slave[c]

        @pl.when(step < STEPS - 1)
        def _():
            for copy in back_copies[:2]:
                copy.start()
            shared = take(part, own_rows, sids[...])
            for c in range(3):
                o_send_m[step, c] = shared[c][:GHOST_ROWS]
                o_send_s[step, c] = shared[c][GHOST_ROWS:]
            for copy in back_copies[4:]:
                copy.start()

        for copy in back_copies[2:4]:
            copy.wait()

        def ghost_sum(values, hot, from_mesh, from_sub):
            for c in range(3):
                for r in range(GHOST_ROWS):
                    values[c : c + 1, r * SEG : (r + 1) * SEG] = from_mesh[step, c, r : r + 1]
                    at = (GHOST_ROWS + r) * SEG
                    values[c : c + 1, at : at + SEG] = from_sub[step, c, r : r + 1]
            top = values[...].astype(BF16).astype(F32)
            both = jnp.concatenate([top, values[...] - top], axis=0).astype(BF16)
            total = dot_nt(both, hot[...])
            return total[:8] + total[8:]

        @pl.when(step < STEPS - 1)
        def _():
            for copy in back_copies[:2] + back_copies[4:]:
                copy.wait()
            sum_m = ghost_sum(values_m, same_m, f_send_m, x_recv_s)
            sum_s = ghost_sum(values_s, same_s, x_recv_m, f_send_s)
            for c in range(3):
                rows = [sum_m[c : c + 1, r * SEG : (r + 1) * SEG] for r in range(GHOST_ROWS)]
                rows += [sum_s[c : c + 1, r * SEG : (r + 1) * SEG] for r in range(GHOST_ROWS)]
                owned = jnp.concatenate([o_recv_m[step, c], o_recv_s[step, c]], axis=0)
                total = owned + jnp.concatenate(rows, axis=0)
                vel[c, own_rows:, :] = vel[c, own_rows:, :] + TIME_STEP * total / ghost_mass

        terms = []
        for c in range(3):
            came = jnp.concatenate([f_recv_m[step, c], f_recv_s[step, c]], axis=0)
            tops, lows = [], []
            for r in range(2 * GHOST_ROWS):
                high = lax.shift_right_logical(sids[r : r + 1, :], 7)
                top, low = halves(jnp.where(high_lane == high, came[r : r + 1], 0.0))
                tops.append(top)
                lows.append(low)
            terms.append(jnp.concatenate(tops, axis=1))
            terms.append(jnp.concatenate(lows, axis=1))
        added = dot_nt(jnp.concatenate(terms, axis=0), onehot_back[...])
        for c in range(3):
            own = part[c] + added[c * 32 : c * 32 + own_rows] + added[c * 32 + 16 : c * 32 + 16 + own_rows]
            now = vel[c, :own_rows, :] + TIME_STEP * own / mass[0]
            vel[c, :own_rows, :] = now
            pos[c] = pos[c] + TIME_STEP * now
        whole.wait_send()
        back.wait_send()

        return step_carry

    lax.fori_loop(0, STEPS, one_step, 0)

    def velocity_lanes(row, carry):
        for c in range(3):
            vel_out[pl.ds(c, 1), lanes_of(row)] = vel[c, pl.ds(row, 1), :]
        return carry

    def stress_lanes(row, carry):
        for c in range(3):
            stress_out[pl.ds(c, 1), lanes_of(row)] = snow[c, pl.ds(row, 1), :]
        return carry

    lax.fori_loop(0, own_rows, velocity_lanes, 0)
    lax.fori_loop(0, blocks, stress_lanes, 0)


def per_device(
    coords, veloc, node_mass, stress, connect, send_mesh, send_sub, send_pick, bucket_list, pair_mask
):
    peers = lax.axis_size("mesh")
    nodes = coords.shape[1]
    elems = stress.shape[1]
    own_rows, blocks = nodes // SEG, elems // SEG
    cands = bucket_list.shape[1]
    slots = send_pick.shape[1]
    pairs = cands * own_rows
    table_rows = own_rows + 2 * GHOST_ROWS
    in_vmem = pl.BlockSpec(memory_space=pltpu.VMEM)
    in_smem = pl.BlockSpec(memory_space=pltpu.SMEM)
    v = pltpu.VMEM
    return pl.pallas_call(
        functools.partial(kernel, own_rows, blocks, cands),
        out_shape=(
            jax.ShapeDtypeStruct((3, nodes), F32),
            jax.ShapeDtypeStruct((3, elems), F32),
        ),
        in_specs=[in_vmem] * 7 + [in_smem] * 2 + [in_vmem] * 2,
        out_specs=(in_vmem, in_vmem),
        scratch_shapes=[
            v((4, blocks, SEG), jnp.int32),
            v((2 * GHOST_ROWS, SEG), jnp.int32),
            v((3, own_rows, SEG), F32),
            v((3, table_rows, SEG), F32),
            v((1, own_rows, SEG), F32),
            v((4, 3, blocks, SEG), F32),
            v((4, 3, blocks, SEG), F32),
            v((3, blocks, SEG), F32),
            v((3, blocks, SEG), F32),
            v((blocks, SEG), F32),
            v((blocks, 6, SEG), F32),
            v((slots, 6, SEG), F32),
            v((STEPS, slots, 6, SEG), F32),
            v((SEG, 4 * elems), BF16),
            v((SEG, 2 * GHOST_ROWS * SEG), BF16),
            v((32, 4 * elems), BF16),
            *[v((144, 32 * SEG), BF16)] * 2,
            v((4, 3, blocks, SEG), F32),
            v((4, 3, blocks, SEG), F32),
            v((3, table_rows, SEG), F32),
            v((own_rows, SEG, 48), BF16),
            v((cands, own_rows, SEG, SEG), F32),
            v((SEG, cands * 2 * SEG), F32),
            v((SEG, cands * 2 * SEG), F32),
            v((SEG, cands * SEG), BF16),
            v((SEG, cands * SEG), BF16),
            v((16, cands * SEG), BF16),
            v((SEG, cands * SEG), BF16),
            v((SEG, cands * SEG), BF16),
            v((16, cands * SEG), BF16),
            v((pairs * 8, SEG), F32),
            v((pairs * 8, slots), F32),
            v((3, own_rows, SEG), F32),
            v((STEPS, peers, CAP, SEG), F32),
            v((STEPS, peers, CAP, SEG), F32),
            *[v((7, GHOST_ROWS, SEG), F32)] * 4,
            *[v((2 * GHOST_ROWS, SEG), jnp.int32)] * 2,
            *[v((GHOST_ROWS * SEG, 2 * GHOST_ROWS * SEG), BF16)] * 2,
            *[v((8, 2 * GHOST_ROWS * SEG), F32)] * 2,
            v((3, own_rows, SEG), F32),
            *[v((STEPS, 3, GHOST_ROWS, SEG), F32)] * 10,
            pltpu.SemaphoreType.DMA((8 + STEPS * 12,)),
            pltpu.SemaphoreType.DMA((2, STEPS)),
            pltpu.SemaphoreType.DMA((2, STEPS)),
        ],
        compiler_params=pltpu.CompilerParams(
            collective_id=0, has_side_effects=True, vmem_limit_bytes=56 * 1024 * 1024
        ),
    )(
        coords,
        veloc,
        node_mass.reshape(1, nodes),
        stress,
        connect,
        send_mesh.reshape(1, -1),
        send_sub.reshape(1, -1),
        send_pick,
        bucket_list,
        send_pick,
        pair_mask,
    )


def solution(mesh):
    both = ("mesh", "sub")
    return jax.shard_map(
        per_device,
        mesh=mesh,
        in_specs=(
            P(None, both),
            P(None, both),
            P(both),
            P(None, both),
            P(None, both),
            P(both),
            P(both),
            P(None, both),
            P(None, None, both),
            P(None, None, both),
        ),
        out_specs=(P(None, both), P(None, both)),
        check_vma=False,
    )
```
